32 devices in a mesh: dp: 4 (over x, core), row: 4 (over z), col: 2 (over y).
Axes of the slice: x: 2, y: 2, z: 4, core: 2. Of those that a mesh axis runs over, the one named last changes fastest.
Arguments:
- tokens_in: bfloat16 [8192, 768], P(('dp', 'col'), 'row'), may hold values from -6 to 6
- out_cot: bfloat16 [8192, 768], P(('dp', 'col'), 'row'), may hold values from -6 to 6
- segments: int32 [16, 512], P('dp'), may hold values from 0 to 31, never falling along the last dimension, each value on 1 to 256 neighbouring positions
- norm_params: float32 [4, 768], P(None, 'row'), may hold values from -1.2 to 1.5, as said below
- qkv_weight: float32 [768, 2304], P('row', 'col'), may hold values from -0.21875 to 0.21875
- proj_weight: float32 [768, 768], P('col', 'row'), may hold values from -0.875 to 0.875
- up_weight: float32 [768, 3072], P('row', 'col'), may hold values from -0.21875 to 0.21875
- down_weight: float32 [3072, 768], P('col', 'row'), may hold values from -0.109375 to 0.109375
- norm_first: float32 [4, 768], P(None, 'row'), may hold values from -18 to 18
- norm_second: float32 [4, 768], P(None, 'row'), may hold values from 30 to 300
- qkv_first: float32 [768, 2304], P('row', 'col'), may hold values from -18 to 18
- qkv_second: float32 [768, 2304], P('row', 'col'), may hold values from 30 to 300
- proj_first: float32 [768, 768], P('col', 'row'), may hold values from -18 to 18
- proj_second: float32 [768, 768], P('col', 'row'), may hold values from 30 to 300
- up_first: float32 [768, 3072], P('row', 'col'), may hold values from -18 to 18
- up_second: float32 [768, 3072], P('row', 'col'), may hold values from 30 to 300
- down_first: float32 [3072, 768], P('col', 'row'), may hold values from -18 to 18
- down_second: float32 [3072, 768], P('col', 'row'), may hold values from 30 to 300
Outputs:
- output: bfloat16 [8192, 768], P(('dp', 'col'), 'row')
- input_grad: bfloat16 [8192, 768], P(('dp', 'col'), 'row')
- norm_grad: float32 [4, 768], P(None, 'row')
- qkv_grad: float32 [768, 2304], P('row', 'col')
- proj_grad: float32 [768, 768], P('col', 'row')
- up_grad: float32 [768, 3072], P('row', 'col')
- down_grad: float32 [3072, 768], P('col', 'row')
- norm_new: float32 [4, 768], P(None, 'row')
- qkv_new: float32 [768, 2304], P('row', 'col')
- proj_new: float32 [768, 768], P('col', 'row')
- up_new: float32 [768, 3072], P('row', 'col')
- down_new: float32 [3072, 768], P('col', 'row')
- norm_first_new: float32 [4, 768], P(None, 'row')
- norm_second_new: float32 [4, 768], P(None, 'row')
- qkv_first_new: float32 [768, 2304], P('row', 'col')
- qkv_second_new: float32 [768, 2304], P('row', 'col')
- proj_first_new: float32 [768, 768], P('col', 'row')
- proj_second_new: float32 [768, 768], P('col', 'row')
- up_first_new: float32 [768, 3072], P('row', 'col')
- up_second_new: float32 [768, 3072], P('row', 'col')
- down_first_new: float32 [3072, 768], P('col', 'row')
- down_second_new: float32 [3072, 768], P('col', 'row')
The draws below stay inside these ranges and needn't reach their ends.
Inputs may be any that keep to these rules, and one draw needn't show every extreme that they name: `segments`: within a row the numbers never fall; no number covers more than 256 positions of a row, and one covers exactly that many. `norm_params`: rows 0 and 2 lie in 0.5 to 1.5.
All inputs are finite; a program needn't handle non-finite values.
Results may differ from the reference program's by a relative error of at most 0.0093.
Values may be sent and summed in bfloat16 or wider, within the bound.
A program may use at most 192 MiB of HBM per device.

```python
import math
import jax
import jax.numpy as jnp
import numpy as np
from jax import lax

D = 768
HEADS = 12
HEAD_DIM = 64
ROT_DIM = 16
FF = 3072
SEQ_LEN = 512
STEP = 3
SEQUENCES = 16
TOKENS = 8192


def draw_norm_params(key, part):
    gain_key, bias_key = jax.random.split(key)
    gains = jax.random.uniform(gain_key, (2, D), jnp.float32, 0.5, 1.5)
    biases = jnp.clip(0.3 * jax.random.normal(bias_key, (2, D), jnp.float32), -1.2, 1.2)
    return jnp.stack([gains[0], biases[0], gains[1], biases[1]], 0)


def levels(stream_key, shape, cuts, least, high):
    gain = 1.0
    for dim, parts in cuts:
        draws = jax.random.uniform(jax.random.fold_in(jax.random.fold_in(stream_key, 6), dim), (parts,), jnp.float32, least / len(cuts), high / len(cuts))
        gain = gain * jnp.repeat(jnp.exp(draws), shape[dim] // parts).reshape((-1,) + (1,) * (len(shape) - 1 - dim))
    return gain


def profile(count, total, most, slope):
    portions = [(1 << 20) // math.isqrt(standing ** slope) + 1 for standing in range(2, count + 1)]
    surplus, holding = total - most - (count - 1), [1] * (count - 1)
    while surplus > 0:
        movable = [i for i in range(count - 1) if holding[i] < most]
        mass, left = sum([portions[i] for i in movable]), surplus
        for i in movable:
            more = min(most - holding[i], max(1, left * portions[i] // mass), surplus)
            holding[i] = holding[i] + more
            surplus = surplus - more
    return np.array([most] + holding)


def uneven(key, amount, total, bound, lean):
    if amount == 2:
        one = jax.random.randint(key, (), max(1, total - bound), min(bound, total - 1) + 1)
        return jnp.stack([one, total - one])
    sizes = jnp.asarray(profile(amount, total, bound, lean), jnp.int32)
    couples = (amount - 1) // 2
    giver, sink = sizes[1:1 + 2 * couples:2], sizes[2:2 + 2 * couples:2]
    margin = jnp.minimum(giver - 1, bound - sink)
    passed = jax.random.randint(jax.random.fold_in(key, 1), (couples,), 0, 1 << 20) % (margin + 1)
    sizes = sizes.at[1:1 + 2 * couples:2].set(giver - passed).at[2:2 + 2 * couples:2].set(sink + passed)
    return sizes[jax.random.permutation(jax.random.fold_in(key, 2), amount)]


def bell_draw(own_key, shape, scale, reach, cuts=(), kind=jnp.bfloat16):
    gain = levels(own_key, shape, cuts, -0.22, 0.18) if cuts else 1.0
    drawn = jax.random.normal(own_key, shape, jnp.float32) * scale * gain
    return jnp.minimum(jnp.maximum(drawn, -reach), reach).astype(kind)


def setup_inputs(seed: int = 0) -> dict:
    seeds = jax.random.split(jax.random.key(seed), 19)
    tokens_in = bell_draw(seeds[0], (TOKENS, D), 1.0, 6.0, ((0, 8), (1, 4)))
    out_cot = bell_draw(seeds[1], (TOKENS, D), 1.0, 6.0, ((0, 8), (1, 4)))
    segments = jax.vmap(lambda own: jnp.searchsorted(jnp.cumsum(uneven(own, SEQ_LEN // 16, SEQ_LEN, SEQ_LEN // 2, 2)), jnp.arange(SEQ_LEN), side="right"))(jax.random.split(seeds[2], SEQUENCES)).reshape((SEQUENCES, SEQ_LEN)).astype(jnp.int32)
    norm_params = draw_norm_params(jax.random.fold_in(seeds[18], 71), 0)
    qkv_weight = bell_draw(seeds[4], (D, 3 * D), D ** -0.5, 0.21875, ((0, 4), (1, 2)), jnp.float32)
    proj_weight = bell_draw(seeds[5], (D, D), (D // 16) ** -0.5, 0.875, ((0, 2), (1, 4)), jnp.float32)
    up_weight = bell_draw(seeds[6], (D, FF), D ** -0.5, 0.21875, ((0, 4), (1, 2)), jnp.float32)
    down_weight = bell_draw(seeds[7], (FF, D), FF ** -0.5, 0.109375, ((0, 2), (1, 4)), jnp.float32)
    norm_first = bell_draw(seeds[8], (4, D), 3.0, 18.0, ((1, 4),), jnp.float32)
    norm_second = jnp.clip(jnp.exp(math.log(300.0) - 2.3025851 * jax.random.uniform(seeds[9], (4, D), jnp.float32) ** levels(seeds[9], (4, D), ((1, 4),), -0.2, 0.2)), 30.0, 300.0)
    qkv_first = bell_draw(seeds[10], (D, 3 * D), 3.0, 18.0, ((0, 4), (1, 2)), jnp.float32)
    qkv_second = jnp.clip(jnp.exp(math.log(300.0) - 2.3025851 * jax.random.uniform(seeds[11], (D, 3 * D), jnp.float32) ** levels(seeds[11], (D, 3 * D), ((0, 4), (1, 2)), -0.2, 0.2)), 30.0, 300.0)
    proj_first = bell_draw(seeds[12], (D, D), 3.0, 18.0, ((0, 2), (1, 4)), jnp.float32)
    proj_second = jnp.clip(jnp.exp(math.log(300.0) - 2.3025851 * jax.random.uniform(seeds[13], (D, D), jnp.float32) ** levels(seeds[13], (D, D), ((0, 2), (1, 4)), -0.2, 0.2)), 30.0, 300.0)
    up_first = bell_draw(seeds[14], (D, FF), 3.0, 18.0, ((0, 4), (1, 2)), jnp.float32)
    up_second = jnp.clip(jnp.exp(math.log(300.0) - 2.3025851 * jax.random.uniform(seeds[15], (D, FF), jnp.float32) ** levels(seeds[15], (D, FF), ((0, 4), (1, 2)), -0.2, 0.2)), 30.0, 300.0)
    down_first = bell_draw(seeds[16], (FF, D), 3.0, 18.0, ((0, 2), (1, 4)), jnp.float32)
    down_second = jnp.clip(jnp.exp(math.log(300.0) - 2.3025851 * jax.random.uniform(seeds[17], (FF, D), jnp.float32) ** levels(seeds[17], (FF, D), ((0, 2), (1, 4)), -0.2, 0.2)), 30.0, 300.0)
    return {"tokens_in": tokens_in, "out_cot": out_cot, "segments": segments, "norm_params": norm_params, "qkv_weight": qkv_weight, "proj_weight": proj_weight, "up_weight": up_weight, "down_weight": down_weight, "norm_first": norm_first, "norm_second": norm_second, "qkv_first": qkv_first, "qkv_second": qkv_second, "proj_first": proj_first, "proj_second": proj_second, "up_first": up_first, "up_second": up_second, "down_first": down_first, "down_second": down_second}


norm_eps = 1e-05
rotary_base = 10000.0
learn_rate = 0.01
beta_first = 0.9
beta_second = 0.95
adam_eps = 1e-08
decay_rate = 0.1
mask_fill = -1e+30
inv_sqrt_two = 0.7071067811865476
inv_sqrt_two_pi = 0.3989422804014327

def gelu_value(value):
    return 0.5 * value * (1.0 + lax.erf(value * inv_sqrt_two))

def gelu_slope(value):
    return 0.5 * (1.0 + lax.erf(value * inv_sqrt_two)) + value * inv_sqrt_two_pi * jnp.exp(-0.5 * value * value)

def positions_of(segs):
    length = segs.shape[-1]
    index = jnp.broadcast_to(jnp.arange(length, dtype=jnp.int32), segs.shape)
    starts = jnp.concatenate([jnp.ones(segs.shape[:-1] + (1,), bool), segs[..., 1:] != segs[..., :-1]], -1)
    first = lax.cummax(jnp.where(starts, index, 0).astype(jnp.int32), axis=segs.ndim - 1)
    return index - first

def rotary_tables(positions):
    half = ROT_DIM // 2
    freq = rotary_base ** (-2.0 * jnp.arange(half, dtype=jnp.float32) / ROT_DIM)
    angle = positions.astype(jnp.float32)[..., None] * freq
    return (jnp.cos(angle), jnp.sin(angle))

def rotate(tensor, cosine, sine):
    half = ROT_DIM // 2
    cos_part = cosine[..., None, :]
    sin_part = sine[..., None, :]
    front = tensor[..., :half]
    back = tensor[..., half:ROT_DIM]
    return jnp.concatenate([front * cos_part - back * sin_part, back * cos_part + front * sin_part, tensor[..., ROT_DIM:]], -1)

def rotate_back(grad, cosine, sine):
    half = ROT_DIM // 2
    cos_part = cosine[..., None, :]
    sin_part = sine[..., None, :]
    front = grad[..., :half]
    back = grad[..., half:ROT_DIM]
    return jnp.concatenate([front * cos_part + back * sin_part, back * cos_part - front * sin_part, grad[..., ROT_DIM:]], -1)

def masked_scores(query, keys, segment):
    length = segment.shape[0]
    scores = jnp.einsum('qhd,khd->hqk', query.astype(jnp.float32), keys.astype(jnp.float32)) / math.sqrt(HEAD_DIM)
    index = jnp.arange(length, dtype=jnp.int32)
    allowed = (segment[:, None] == segment[None, :]) & (index[None, :] <= index[:, None])
    return jnp.where(allowed[None], scores, mask_fill)

def attend(query, keys, values, segment):
    scores = masked_scores(query, keys, segment)
    total = lax.optimization_barrier(jnp.sum(jnp.exp(scores), -1, keepdims=True))
    logsum = jnp.log(total)
    weights = jnp.exp(scores - logsum).astype(jnp.bfloat16)
    mixed = jnp.einsum('hqk,khd->qhd', weights.astype(jnp.float32), values.astype(jnp.float32)).astype(jnp.bfloat16)
    return (mixed, logsum[..., 0])

def attend_back(query, keys, values, segment, logsum, mixed, grad_mixed):
    scores = masked_scores(query, keys, segment)
    probs = jnp.exp(scores - logsum[..., None])
    weights = probs.astype(jnp.bfloat16).astype(jnp.float32)
    grad_f = grad_mixed.astype(jnp.float32)
    value_grad = jnp.einsum('hqk,qhd->khd', weights, grad_f)
    prod_grad = jnp.einsum('qhd,khd->hqk', grad_f, values.astype(jnp.float32))
    delta = lax.optimization_barrier(jnp.sum(grad_f * mixed.astype(jnp.float32), -1)).T
    score_grad = (probs * (prod_grad - delta[..., None]) / math.sqrt(HEAD_DIM)).astype(jnp.bfloat16).astype(jnp.float32)
    query_grad = jnp.einsum('hqk,khd->qhd', score_grad, keys.astype(jnp.float32))
    key_grad = jnp.einsum('hqk,qhd->khd', score_grad, query.astype(jnp.float32))
    return (query_grad, key_grad, value_grad)

def dot32(left, right):
    return jnp.dot(left, right, preferred_element_type=jnp.float32)

def run_block(tokens, cotan, segs, gains, qkv16, proj16, up16, down16):
    count = tokens.shape[0]
    nseq = segs.shape[0]
    xfull = tokens.astype(jnp.float32)
    mean = lax.optimization_barrier(jnp.mean(xfull, -1, keepdims=True))
    spread = lax.optimization_barrier(jnp.mean(xfull * xfull, -1, keepdims=True)) - mean * mean
    rstd = lax.rsqrt(spread + norm_eps)
    normed = (xfull - mean) * rstd
    first_in = (normed * gains[0] + gains[1]).astype(jnp.bfloat16)
    second_in = (normed * gains[2] + gains[3]).astype(jnp.bfloat16)
    packed = dot32(first_in, qkv16).reshape(nseq, SEQ_LEN, HEADS, 3, HEAD_DIM)
    cosine, sine = rotary_tables(positions_of(segs))
    query = rotate(packed[..., 0, :], cosine, sine).astype(jnp.bfloat16)
    keys = rotate(packed[..., 1, :], cosine, sine).astype(jnp.bfloat16)
    values = packed[..., 2, :].astype(jnp.bfloat16)
    attended, logsum = lax.map(lambda item: attend(*item), (query, keys, values, segs))
    attended_flat = attended.reshape(count, D)
    hidden = dot32(second_in, up16)
    active = gelu_value(hidden).astype(jnp.bfloat16)
    output = (xfull + dot32(attended_flat, proj16) + dot32(active, down16)).astype(jnp.bfloat16)
    proj_grad = dot32(attended_flat.T, cotan)
    down_grad = dot32(active.T, cotan)
    attended_grad = dot32(cotan, proj16.T).astype(jnp.bfloat16)
    hidden_grad = (dot32(cotan, down16.T) * gelu_slope(hidden)).astype(jnp.bfloat16)
    grad_heads = attended_grad.reshape(nseq, SEQ_LEN, HEADS, HEAD_DIM)
    query_grad, key_grad, value_grad = lax.map(lambda item: attend_back(*item), (query, keys, values, segs, logsum, attended, grad_heads))
    query_grad = rotate_back(query_grad, cosine, sine)
    key_grad = rotate_back(key_grad, cosine, sine)
    packed_grad = jnp.stack([query_grad, key_grad, value_grad], 3).reshape(count, 3 * D).astype(jnp.bfloat16)
    qkv_grad = dot32(first_in.T, packed_grad)
    up_grad = dot32(second_in.T, hidden_grad)
    first_grad = dot32(packed_grad, qkv16.T)
    second_grad = dot32(hidden_grad, up16.T)
    norm_grad = jnp.stack([lax.optimization_barrier(jnp.sum(first_grad * normed, 0)), lax.optimization_barrier(jnp.sum(first_grad, 0)), lax.optimization_barrier(jnp.sum(second_grad * normed, 0)), lax.optimization_barrier(jnp.sum(second_grad, 0))], 0)
    combined = gains[0] * first_grad + gains[2] * second_grad
    input_grad = (cotan.astype(jnp.float32) + rstd * (combined - lax.optimization_barrier(jnp.mean(combined, -1, keepdims=True)) - normed * lax.optimization_barrier(jnp.mean(combined * normed, -1, keepdims=True)))).astype(jnp.bfloat16)
    return (output, input_grad, (norm_grad, qkv_grad, proj_grad, up_grad, down_grad))

def adam_update(weight, first, second, grad, decay):
    first_new = beta_first * first + (1.0 - beta_first) * grad
    second_new = beta_second * second + (1.0 - beta_second) * grad * grad
    first_hat = first_new / (1.0 - beta_first ** STEP)
    second_hat = second_new / (1.0 - beta_second ** STEP)
    weight_new = weight - learn_rate * (first_hat / (jnp.sqrt(second_hat) + adam_eps) + decay * weight)
    return (weight_new, first_new, second_new)

def reference(tokens_in, out_cot, segments, norm_params, qkv_weight, proj_weight, up_weight, down_weight, norm_first, norm_second, qkv_first, qkv_second, proj_first, proj_second, up_first, up_second, down_first, down_second):
    qkv16 = qkv_weight.astype(jnp.bfloat16)
    proj16 = proj_weight.astype(jnp.bfloat16)
    up16 = up_weight.astype(jnp.bfloat16)
    down16 = down_weight.astype(jnp.bfloat16)
    block_seqs = math.gcd(SEQUENCES, 8)
    blocks = SEQUENCES // block_seqs
    tok_blocks = tokens_in.reshape(blocks, block_seqs * SEQ_LEN, D)
    cot_blocks = out_cot.reshape(blocks, block_seqs * SEQ_LEN, D)
    seg_blocks = segments.reshape(blocks, block_seqs, SEQ_LEN)
    zeros = (jnp.zeros((4, D), jnp.float32), jnp.zeros((D, 3 * D), jnp.float32), jnp.zeros((D, D), jnp.float32), jnp.zeros((D, FF), jnp.float32), jnp.zeros((FF, D), jnp.float32))

    def scan_step(carry, item):
        output, input_grad, grads = run_block(item[0], item[1], item[2], norm_params, qkv16, proj16, up16, down16)
        carry = jax.tree.map(lambda total, part: total + part, carry, grads)
        return (carry, (output, input_grad))
    grads, outs = lax.scan(scan_step, zeros, (tok_blocks, cot_blocks, seg_blocks))
    output = outs[0].reshape(TOKENS, D)
    input_grad = outs[1].reshape(TOKENS, D)
    norm_grad, qkv_grad, proj_grad, up_grad, down_grad = grads
    norm_new, norm_first_new, norm_second_new = adam_update(norm_params, norm_first, norm_second, norm_grad, 0.0)
    qkv_new, qkv_first_new, qkv_second_new = adam_update(qkv_weight, qkv_first, qkv_second, qkv_grad, decay_rate)
    proj_new, proj_first_new, proj_second_new = adam_update(proj_weight, proj_first, proj_second, proj_grad, decay_rate)
    up_new, up_first_new, up_second_new = adam_update(up_weight, up_first, up_second, up_grad, decay_rate)
    down_new, down_first_new, down_second_new = adam_update(down_weight, down_first, down_second, down_grad, decay_rate)
    return (output, input_grad, norm_grad, qkv_grad, proj_grad, up_grad, down_grad, norm_new, qkv_new, proj_new, up_new, down_new, norm_first_new, norm_second_new, qkv_first_new, qkv_second_new, proj_first_new, proj_second_new, up_first_new, up_second_new, down_first_new, down_second_new)
```

```python
import functools
import math

import jax
import jax.numpy as jnp
from jax import lax
from jax.experimental import pallas as pl
from jax.experimental.pallas import tpu as pltpu
from jax.sharding import PartitionSpec as P

D = 768
HEAD_DIM = 64
ROT_DIM = 16
SEQ_LEN = 512
STEP = 3


norm_eps = 1e-05
rotary_base = 10000.0
learn_rate = 0.01
beta_first = 0.9
beta_second = 0.95
adam_eps = 1e-08
decay_rate = 0.1
mask_fill = -1e30
inv_sqrt_two = 0.7071067811865476
inv_sqrt_two_pi = 0.3989422804014327


def adam_update(weight, first, second, grad, decay):
    first_new = beta_first * first + (1.0 - beta_first) * grad
    second_new = beta_second * second + (1.0 - beta_second) * grad * grad
    first_hat = first_new / (1.0 - beta_first**STEP)
    second_hat = second_new / (1.0 - beta_second**STEP)
    weight_new = weight - learn_rate * (
        first_hat / (jnp.sqrt(second_hat) + adam_eps) + decay * weight
    )
    return (weight_new, first_new, second_new)


MESH = pl.DeviceIdType.MESH
LANES = 128
QUARTERS = 4
WINDOW = 256
QBLOCK = 128


def remote(src, dst, send_sem, recv_sem, device):
    return pltpu.make_async_remote_copy(
        src_ref=src,
        dst_ref=dst,
        send_sem=send_sem,
        recv_sem=recv_sem,
        device_id=device,
        device_id_type=MESH,
    )


def places(row_count):
    data, row, col = lax.axis_index("dp"), lax.axis_index("row"), lax.axis_index("col")
    quarter = lax.rem(data, QUARTERS)
    far = data - quarter + lax.rem(quarter + 2, QUARTERS)
    mate = data + 1 - 2 * lax.rem(quarter, 2)
    return data, row, col, quarter, far, mate


def greet(peers):
    barrier = pltpu.get_barrier_semaphore()
    for peer in peers:
        pl.semaphore_signal(barrier, inc=1, device_id=peer, device_id_type=MESH)
    pl.semaphore_wait(barrier, len(peers))


def gather_kernel(row_count, tok, cot, nrm, w0, w1, w2, xg, cg, ng, g0, g1, g2, hop, *sems):
    (nrm_s, nrm_r, x_s, x_r, xy_s, xy_r, h_s, h_r, c_s, c_r, cy_s, cy_r, loc,
     z_s, z_r, f_s, f_r, m_s, m_r) = sems
    data, row, col, quarter, far, mate = places(row_count)
    shares = tok.shape[0]
    other = 1 - col
    home = row // shares
    own_w, all_w = (w0, w1, w2), (g0, g1, g2)
    groups = len(own_w)
    depth = w0.shape[0] // QUARTERS
    others = [lax.rem(row + k, row_count) for k in range(1, row_count)]
    greet(
        [(data, t, col) for t in others]
        + [(data, row, other), (far, row, col), (mate, row, col)]
    )

    def rows(part):
        return pl.ds(pl.multiple_of(part * depth, depth), depth)

    def step_copy(g, src, up):
        at = all_w[g].at[src, rows(quarter)]
        return remote(at, at, z_s.at[int(up), g, src], z_r.at[g, src],
                      (data, row + 1 if up else row - 1, col))

    def own_copy(g, up):
        return remote(own_w[g].at[rows(quarter)], all_w[g].at[row, rows(quarter)],
                      z_s.at[int(up), g, row], z_r.at[g, row],
                      (data, row + 1 if up else row - 1, col))

    def far_copy(g, src):
        at = all_w[g].at[src, rows(quarter)]
        return remote(at, at, f_s.at[g, src], f_r.at[g, src], (far, row, col))

    def far_wait(g, src):
        at = all_w[g].at[src, rows(lax.rem(quarter + 2, QUARTERS))]
        remote(at, at, f_s.at[g, src], f_r.at[g, src], (far, row, col)).wait_recv()

    def mate_copy(g, src, second):
        part = lax.rem(quarter + 2, QUARTERS) if second else quarter
        at = all_w[g].at[src, rows(part)]
        return remote(at, at, m_s.at[int(second), g, src], m_r.at[int(second), g, src],
                      (mate, row, col))

    def mate_wait(g, src, second):
        theirs = quarter + 1 - 2 * lax.rem(quarter, 2)
        part = lax.rem(theirs + 2, QUARTERS) if second else theirs
        at = all_w[g].at[src, rows(part)]
        remote(at, at, m_s.at[int(second), g, src], m_r.at[int(second), g, src],
               (mate, row, col)).wait_recv()

    def norm_copy(k):
        return remote(nrm, ng.at[row], nrm_s.at[k], nrm_r.at[row], (data, others[k], col))

    def norm_wait(k):
        remote(nrm, ng.at[others[k]], nrm_s.at[k], nrm_r.at[others[k]],
               (data, others[k], col)).wait_recv()

    def token_copy(j):
        return remote(tok.at[j], xg.at[row], x_s.at[j], x_r.at[row],
                      (data, col * shares + j, col))

    def token_local(j):
        return pltpu.make_async_copy(tok.at[j], xg.at[row], loc.at[0])

    def hop_copy(j):
        return remote(cot.at[j], hop.at[j], h_s.at[j], h_r.at[j], (data, row, other))

    def cot_copy(j):
        return remote(hop.at[j], cg.at[row], c_s.at[j], c_r.at[row],
                      (data, other * shares + j, col))

    def cot_local(j):
        return pltpu.make_async_copy(hop.at[j], cg.at[row], loc.at[1])

    def x_wait(src):
        remote(tok.at[0], xg.at[src], x_s.at[0], x_r.at[src], (data, src, col)).wait_recv()

    def c_wait(src):
        remote(tok.at[0], cg.at[src], c_s.at[0], c_r.at[src], (data, src, col)).wait_recv()

    def across(ref, sems_, src):
        return remote(ref.at[src], ref.at[src], sems_[0].at[src], sems_[1].at[src],
                      (data, row, other))

    x_main = col == home
    c_main = col != home

    for k in range(row_count - 1):
        norm_copy(k).start()
    own_norm = pltpu.make_async_copy(nrm, ng.at[row], loc.at[2])
    own_norm.start()
    for j in range(shares):
        @pl.when(col * shares + j != row)
        def _():
            token_copy(j).start()

        @pl.when(col * shares + j == row)
        def _():
            token_local(j).start()
        hop_copy(j).start()

    def send_own(g):
        @pl.when(row + 1 < row_count)
        def _():
            own_copy(g, True).start()

        @pl.when(row > 0)
        def _():
            own_copy(g, False).start()

    pending = []

    def settle():
        for g, k, below in pending:
            src = row - k if below else row + k

            @pl.when(src >= 0 if below else src < row_count)
            def _():
                far_wait(g, src)
                mate_copy(g, src, True).start()
        pending.clear()

    def relay(g):
        for k in range(1, row_count):
            now = []
            for below in (True, False):
                src = row - k if below else row + k

                @pl.when(src >= 0 if below else src < row_count)
                def _():
                    step_copy(g, src, below).wait_recv()
                    onward = row + 1 < row_count if below else row > 0

                    @pl.when(onward)
                    def _():
                        step_copy(g, src, below).start()
                    far_copy(g, src).start()
                    mate_copy(g, src, False).start()
                now.append((g, k, below))
            settle()
            pending.extend(now)

    send_own(0)
    send_own(1)
    for j in range(shares):
        hop_copy(j).wait_recv()

        @pl.when(other * shares + j != row)
        def _():
            cot_copy(j).start()

        @pl.when(other * shares + j == row)
        def _():
            cot_local(j).start()

    @pl.when(x_main)
    def _():
        token_local(0).wait()
        across(xg, (xy_s, xy_r), row).start()
        for src in others:
            x_wait(src)
            across(xg, (xy_s, xy_r), src).start()

    relay(0)
    send_own(2)

    @pl.when(c_main)
    def _():
        cot_local(0).wait()
        across(cg, (cy_s, cy_r), row).start()
        for src in others:
            c_wait(src)
            across(cg, (cy_s, cy_r), src).start()

    for g in range(1, groups):
        relay(g)
    settle()

    for main, ref, pair in ((x_main, xg, (xy_s, xy_r)), (c_main, cg, (cy_s, cy_r))):
        @pl.when(main)
        def _():
            for src in range(row_count):
                across(ref, pair, src).wait_send()

        @pl.when(jnp.logical_not(main))
        def _():
            for src in range(row_count):
                across(ref, pair, src).wait_recv()
    own_norm.wait()
    for k in range(row_count - 1):
        norm_copy(k).wait_send()
        norm_wait(k)
    for j in range(shares):
        @pl.when(col * shares + j != row)
        def _():
            token_copy(j).wait_send()

        @pl.when(other * shares + j != row)
        def _():
            cot_copy(j).wait_send()
        hop_copy(j).wait_send()
    for g in range(groups):
        @pl.when(row + 1 < row_count)
        def _():
            own_copy(g, True).wait_send()

        @pl.when(row > 0)
        def _():
            own_copy(g, False).wait_send()
        for k in range(1, row_count):
            for below in (True, False):
                src = row - k if below else row + k

                @pl.when(src >= 0 if below else src < row_count)
                def _():
                    onward = row + 1 < row_count if below else row > 0

                    @pl.when(onward)
                    def _():
                        step_copy(g, src, below).wait_send()
                    far_copy(g, src).wait_send()
                    for second in (False, True):
                        mate_copy(g, src, second).wait_send()
                        mate_wait(g, src, second)


def gather_all(row_count, tok, cot, nrm, weights):
    shares, packed, _ = tok.shape
    bf16 = jnp.bfloat16
    groups = len(weights)
    dma = pltpu.SemaphoreType.DMA
    anywhere = pl.BlockSpec(memory_space=pl.ANY)
    vmem = pl.BlockSpec(memory_space=pltpu.VMEM)
    n = row_count
    sent = sum(w.size for w in weights) * 2 + tok.size * 8
    return pl.pallas_call(
        functools.partial(gather_kernel, row_count),
        out_shape=[
            jax.ShapeDtypeStruct((n, packed, LANES), bf16),
            jax.ShapeDtypeStruct((n, packed, LANES), bf16),
            jax.ShapeDtypeStruct((n,) + nrm.shape, jnp.float32),
        ] + [jax.ShapeDtypeStruct((n,) + w.shape, bf16) for w in weights],
        in_specs=[anywhere] * (3 + groups),
        out_specs=[vmem] * 3 + [anywhere] * groups,
        scratch_shapes=[
            pltpu.VMEM(tok.shape, bf16),
            dma((n,)), dma((n,)),
            dma((shares,)), dma((n,)), dma((n,)), dma((n,)),
            dma((shares,)), dma((shares,)),
            dma((shares,)), dma((n,)), dma((n,)), dma((n,)),
            dma((3,)),
            dma((2, groups, n)), dma((groups, n)),
            dma((groups, n)), dma((groups, n)),
            dma((2, groups, n)), dma((2, groups, n)),
        ],
        compiler_params=pltpu.CompilerParams(
            collective_id=0, has_side_effects=True, vmem_limit_bytes=16 << 20
        ),
        cost_estimate=pl.CostEstimate(flops=0, bytes_accessed=sent, transcendentals=0),
        name="gather",
    )(tok, cot, nrm, *weights)


def reduce_kernel(row_count, groups_out, outp, gradp, nrmp, p0, p1, p2,
                  out_t, grad_t, nrm_t, r0, r1, r2, *scratch):
    (oy, od, gy, gd, gh, nz, nc, nd, nrm1, nrm2,
     c0, c1, c2, fs0, fs1, fs2, fr0, fr1, fr2, zs0, zs1, zs2, zr0, zr1, zr2, ex0, ex1, ex2,
     oy_s, oy_r, oz_s, oz_r, gy_s, gy_r, gz_s, gz_r, gh_s, gh_r,
     nz_s, nz_r, nc_s, nc_r, nd_s, nd_r,
     c_s, c_r, f_s, f_r, z_s, z_r, e_s, e_r, a_s, a_r, b_s, b_r, loc) = scratch
    data, row, col, quarter, far, mate = places(row_count)
    parts, total = (p0, p1, p2), (r0, r1, r2)
    crecv, fsend, frecv = (c0, c1, c2), (fs0, fs1, fs2), (fr0, fr1, fr2)
    zsend, zrecv, extra = (zs0, zs1, zs2), (zr0, zr1, zr2), (ex0, ex1, ex2)
    groups = len(parts)
    shares = out_t.shape[0]
    other = 1 - col
    home = row // shares
    depth = parts[0].shape[1] // QUARTERS
    data_count = QUARTERS * groups_out
    others = [lax.rem(row + k, row_count) for k in range(1, row_count)]
    order = others + [row]
    wider = [lax.rem(data + QUARTERS * k, data_count) for k in range(1, groups_out)]
    everyone = [lax.rem(data + k, data_count) for k in range(1, data_count)]
    greet([(data, t, col) for t in others] + [(data, row, other)]
          + [(t, row, col) for t in everyone])
    f32, bf16 = jnp.float32, jnp.bfloat16
    half = lax.rem(quarter + 2, QUARTERS)
    theirs = quarter + 1 - 2 * lax.rem(quarter, 2)
    theirs_half = lax.rem(theirs + 2, QUARTERS)

    def rows(part):
        return pl.ds(pl.multiple_of(part * depth, depth), depth)

    def norm_z(k):
        return remote(nrmp.at[others[k]], nz.at[row], nz_s.at[k], nz_r.at[row],
                      (data, others[k], col))

    def norm_z_wait(k):
        remote(nrmp.at[0], nz.at[others[k]], nz_s.at[k], nz_r.at[others[k]],
               (data, others[k], col)).wait_recv()

    def norm_c():
        return remote(nrm1, nc, nc_s, nc_r, (data, row, other))

    def norm_d(k):
        return remote(nrm2, nd.at[data], nd_s.at[k], nd_r.at[data], (everyone[k], row, col))

    def norm_d_wait(k):
        remote(nrm2, nd.at[everyone[k]], nd_s.at[k], nd_r.at[everyone[k]],
               (everyone[k], row, col)).wait_recv()

    def out_y(t):
        return remote(outp.at[t], oy.at[t], oy_s.at[t], oy_r.at[t], (data, row, other))

    def grad_y(t):
        return remote(gradp.at[t], gy.at[t], gy_s.at[t], gy_r.at[t], (data, row, other))

    slot = row - home * shares

    def out_z(t):
        return remote(od.at[t], out_t.at[slot], oz_s.at[t], oz_r.at[slot], (data, t, col))

    def out_z_wait(j):
        remote(od.at[0], out_t.at[j], oz_s.at[0], oz_r.at[j], (data, row, col)).wait_recv()

    def grad_z(t):
        return remote(gd.at[t], gh.at[slot], gz_s.at[t], gz_r.at[slot], (data, t, col))

    def grad_z_wait(j):
        remote(gd.at[0], gh.at[j], gz_s.at[0], gz_r.at[j], (data, row, col)).wait_recv()

    def grad_h(j):
        return remote(gh.at[j], grad_t.at[j], gh_s.at[j], gh_r.at[j], (data, row, other))

    def mate_part(g, t, second):
        part = theirs_half if second else theirs
        return remote(parts[g].at[t, rows(part)], crecv[g].at[int(second), t],
                      c_s.at[int(second), g, t], c_r.at[int(second), g, t], (mate, row, col))

    def far_part(g, t):
        return remote(fsend[g].at[t], frecv[g].at[t], f_s.at[g, t], f_r.at[g, t],
                      (far, row, col))

    def row_part(g, t):
        return remote(zsend[g].at[t], zrecv[g].at[row], z_s.at[g, t], z_r.at[g, row],
                      (data, t, col))

    def row_wait(g, src):
        remote(zsend[g].at[src], zrecv[g].at[src], z_s.at[g, src], z_r.at[g, src],
               (data, src, col)).wait_recv()

    def wide_part(g, k):
        return remote(total[g].at[rows(quarter)], extra[g].at[data // QUARTERS],
                      e_s.at[g, k], e_r.at[g, data // QUARTERS], (wider[k], row, col))

    def wide_wait(g, k):
        remote(total[g].at[rows(quarter)], extra[g].at[wider[k] // QUARTERS],
               e_s.at[g, k], e_r.at[g, wider[k] // QUARTERS], (wider[k], row, col)).wait_recv()

    def far_sum(g):
        at = total[g].at[rows(quarter)]
        return remote(at, at, a_s.at[g], a_r.at[g], (far, row, col))

    def far_sum_wait(g):
        at = total[g].at[rows(half)]
        remote(at, at, a_s.at[g], a_r.at[g], (far, row, col)).wait_recv()

    def mate_sum(g, second):
        at = total[g].at[rows(half if second else quarter)]
        return remote(at, at, b_s.at[int(second), g], b_r.at[int(second), g], (mate, row, col))

    def mate_sum_wait(g, second):
        at = total[g].at[rows(theirs_half if second else theirs)]
        remote(at, at, b_s.at[int(second), g], b_r.at[int(second), g],
               (mate, row, col)).wait_recv()

    o_main = col == home
    g_main = col != home

    for k in range(row_count - 1):
        norm_z(k).start()

    @pl.when(jnp.logical_not(o_main))
    def _():
        for t in order:
            out_y(t).start()

    @pl.when(jnp.logical_not(g_main))
    def _():
        for t in order:
            grad_y(t).start()
    for g in range(groups):
        for t in order:
            mate_part(g, t, True).start()
        for t in order:
            mate_part(g, t, False).start()

    def stage_far(g, t):
        mate_part(g, t, True).wait_recv()
        own = parts[g][t, rows(half), :].astype(f32)
        fsend[g][t] = (own + crecv[g][1, t].astype(f32)).astype(bf16)
        far_part(g, t).start()

    def stage_row(g, t, own_row):
        mate_part(g, t, False).wait_recv()
        far_part(g, t).wait_recv()
        mine = parts[g][t, rows(quarter), :].astype(f32)
        mine = mine + crecv[g][0, t].astype(f32) + frecv[g][t].astype(f32)
        zsend[g][t] = mine.astype(bf16)
        if not own_row:
            row_part(g, t).start()

    def outputs_out():
        @pl.when(o_main)
        def _():
            for t in order:
                out_y(t).wait_recv()
                od[t] = (outp[t].astype(f32) + oy[t].astype(f32)).astype(bf16)
                if t is row:
                    pltpu.make_async_copy(od.at[t], out_t.at[slot], loc.at[0]).start()
                else:
                    out_z(t).start()

    def outputs_grad():
        @pl.when(g_main)
        def _():
            for t in order:
                grad_y(t).wait_recv()
                gd[t] = (gradp[t].astype(f32) + gy[t].astype(f32)).astype(bf16)
                if t is row:
                    pltpu.make_async_copy(gd.at[t], gh.at[slot], loc.at[1]).start()
                else:
                    grad_z(t).start()

    def grads_home():
        for j in range(shares):
            @pl.when(other * shares + j != row)
            def _():
                grad_z_wait(j)

            @pl.when(other * shares + j == row)
            def _():
                pltpu.make_async_copy(gd.at[row], gh.at[slot], loc.at[1]).wait()
            grad_h(j).start()

    def finish(g):
        acc = zsend[g][row].astype(f32)
        for src in others:
            row_wait(g, src)
            acc = acc + zrecv[g][src].astype(f32)
        total[g][rows(quarter), :] = acc.astype(bf16)
        if wider:
            for k in range(len(wider)):
                wide_part(g, k).start()
            for k in range(len(wider)):
                wide_wait(g, k)
                acc = acc + extra[g][wider[k] // QUARTERS].astype(f32)
            for k in range(len(wider)):
                wide_part(g, k).wait_send()
            total[g][rows(quarter), :] = acc.astype(bf16)
        far_sum(g).start()
        mate_sum(g, False).start()

    pieces = [(g, t) for g in range(groups) for t in order]
    lag = 2
    for n in range(len(pieces) + lag):
        if n < len(pieces):
            stage_far(*pieces[n])
        if n == 1:
            outputs_out()
        if n == 3:
            outputs_grad()
            acc = nrmp[row]
            for k in range(row_count - 1):
                norm_z_wait(k)
                acc = acc + nz[others[k]]
            nrm1[...] = acc
            norm_c().start()
        if n == 6:
            norm_c().wait_recv()
            nrm2[...] = nrm1[...] + nc[...]
            for k in range(len(everyone)):
                norm_d(k).start()
        if n == 8:
            grads_home()
        if n >= lag:
            g, t = pieces[n - lag]
            stage_row(g, t, t is row)
            if (n - lag) % row_count == row_count - 1 and g > 0:
                finish(g - 1)
    finish(groups - 1)
    acc = nrm2[...]
    for k in range(len(everyone)):
        norm_d_wait(k)
        acc = acc + nd[everyone[k]]
    nrm_t[...] = acc
    for g in range(groups):
        far_sum_wait(g)
        mate_sum(g, True).start()

    @pl.when(jnp.logical_not(o_main))
    def _():
        for t in range(row_count):
            out_y(t).wait_send()

    @pl.when(jnp.logical_not(g_main))
    def _():
        for t in range(row_count):
            grad_y(t).wait_send()

    @pl.when(o_main)
    def _():
        pltpu.make_async_copy(od.at[row], out_t.at[slot], loc.at[0]).wait()
        for t in others:
            out_z(t).wait_send()

    @pl.when(g_main)
    def _():
        for t in others:
            grad_z(t).wait_send()
    for j in range(shares):
        @pl.when(col * shares + j != row)
        def _():
            out_z_wait(j)
        grad_h(j).wait()
    for k in range(row_count - 1):
        norm_z(k).wait_send()
    norm_c().wait_send()
    for k in range(len(everyone)):
        norm_d(k).wait_send()
    for g in range(groups):
        for t in range(row_count):
            for second in (False, True):
                mate_part(g, t, second).wait_send()
            far_part(g, t).wait_send()
        for t in others:
            row_part(g, t).wait_send()
        far_sum(g).wait_send()
        for second in (False, True):
            mate_sum(g, second).wait_send()
            mate_sum_wait(g, second)


def reduce_all(row_count, data_count, shares, outp, gradp, nrmp, parts):
    n = row_count
    bf16, f32 = jnp.bfloat16, jnp.float32
    dma = pltpu.SemaphoreType.DMA
    vmem = pl.BlockSpec(memory_space=pltpu.VMEM)
    groups = len(parts)
    groups_out = data_count // QUARTERS
    block = outp.shape[1:]
    small = nrmp.shape[1:]
    depth = parts[0].shape[1] // QUARTERS
    widths = [p.shape[2] for p in parts]

    def each(lead, dtype=bf16):
        return [pltpu.VMEM(lead + (depth, w), dtype) for w in widths]

    return pl.pallas_call(
        functools.partial(reduce_kernel, row_count, groups_out),
        out_shape=[
            jax.ShapeDtypeStruct((shares,) + block, bf16),
            jax.ShapeDtypeStruct((shares,) + block, bf16),
            jax.ShapeDtypeStruct(small, f32),
        ] + [jax.ShapeDtypeStruct((p.shape[1], p.shape[2]), bf16) for p in parts],
        in_specs=[vmem] * (3 + groups),
        out_specs=[vmem] * (3 + groups),
        scratch_shapes=[
            pltpu.VMEM((n,) + block, bf16), pltpu.VMEM((n,) + block, bf16),
            pltpu.VMEM((n,) + block, bf16), pltpu.VMEM((n,) + block, bf16),
            pltpu.VMEM((shares,) + block, bf16),
            pltpu.VMEM((n,) + small, f32), pltpu.VMEM(small, f32),
            pltpu.VMEM((data_count,) + small, f32),
            pltpu.VMEM(small, f32), pltpu.VMEM(small, f32),
            *each((2, n)), *each((n,)), *each((n,)), *each((n,)), *each((n,)),
            *each((groups_out,)),
            dma((n,)), dma((n,)), dma((n,)), dma((shares,)),
            dma((n,)), dma((n,)), dma((n,)), dma((shares,)), dma((shares,)), dma((shares,)),
            dma((n,)), dma((n,)), dma, dma, dma((data_count,)), dma((data_count,)),
            dma((2, groups, n)), dma((2, groups, n)),
            dma((groups, n)), dma((groups, n)),
            dma((groups, n)), dma((groups, n)),
            dma((groups, groups_out)), dma((groups, groups_out)),
            dma((groups,)), dma((groups,)),
            dma((2, groups)), dma((2, groups)), dma((2,)),
        ],
        compiler_params=pltpu.CompilerParams(
            collective_id=1, has_side_effects=True, vmem_limit_bytes=44 << 20
        ),
        cost_estimate=pl.CostEstimate(flops=0, bytes_accessed=1 << 24, transcendentals=0),
        name="reduce",
    )(outp, gradp, nrmp, *parts)


def lane_low(shape):
    return lax.broadcasted_iota(jnp.int32, shape, len(shape) - 1) < HEAD_DIM


def swap(tile):
    return pltpu.roll(tile, HEAD_DIM, 1)


def compute_kernel(row_count, width, seg_ref, freq_ref, xg, cg, ng, w0, w1, w2, a0, a1, a2,
                   outp, gradp, nrmp, gq, gu, go,
                   wq, wu, wo, normed, fi, si, co, fit, sit, cot, dcat, act, hg, pg, comb,
                   dk, dv, sem):
    f32, bf16 = jnp.float32, jnp.bfloat16
    row = lax.axis_index("row")
    length = xg.shape[1] * 2 // 3
    halflen = length // 2
    attn = wq.shape[1] // 3
    hidden = wu.shape[1]
    tail = row_count * LANES
    small = w0.shape[0] - LANES

    def loads(g, src, mine):
        own, gathered, dest = ((w0, a0, wq), (w1, a1, wu), (w2, a2, wo))[g]
        view = own if mine else gathered.at[src]
        return (
            pltpu.make_async_copy(view.at[pl.ds(0, LANES)],
                                  dest.at[pl.ds(src * LANES, LANES)], sem.at[0, g, src]),
            pltpu.make_async_copy(view.at[pl.ds(LANES, small)],
                                  dest.at[pl.ds(tail + src * small, small)], sem.at[1, g, src]),
        )

    for g in (0, 2, 1):
        for src in range(row_count):
            @pl.when(row == src)
            def _():
                for copy in loads(g, src, True):
                    copy.start()

            @pl.when(row != src)
            def _():
                for copy in loads(g, src, False):
                    copy.start()

    def landed(g):
        for src in range(row_count):
            for copy in loads(g, src, False):
                copy.wait()

    low = lane_low((halflen, LANES))

    def tails(ref, pair):
        left = ref[2 * pair, length:, :].astype(f32)
        right = ref[2 * pair + 1, length:, :].astype(f32)
        return jnp.concatenate(
            [jnp.where(low, left, swap(right)), jnp.where(low, swap(left), right)], 0)

    def tiles(ref):
        return [ref[r, :length, :].astype(f32) for r in range(row_count)] + [
            tails(ref, p) for p in range(row_count // 2)]

    xt = tiles(xg)
    mean = sum(jnp.sum(t, 1, keepdims=True) for t in xt) / width
    spread = sum(jnp.sum(t * t, 1, keepdims=True) for t in xt) / width - mean * mean
    rstd = lax.rsqrt(spread + norm_eps)
    low8 = lane_low((8, LANES))

    def norm_tile(n):
        if n < row_count:
            return ng[n, :, :LANES]
        left, right = ng[2 * (n - row_count), :, LANES:], ng[2 * (n - row_count) + 1, :, LANES:]
        return jnp.where(low8, left, swap(right))

    ct = tiles(cg)
    for n in range(len(xt)):
        at = slice(n * LANES, (n + 1) * LANES)
        gain = norm_tile(n)
        value = (xt[n] - mean) * rstd
        normed[:, at] = value
        first = (value * gain[0:1] + gain[1:2]).astype(bf16)
        second = (value * gain[2:3] + gain[3:4]).astype(bf16)
        cotan = ct[n].astype(bf16)
        fi[:, at] = first
        si[:, at] = second
        co[:, at] = cotan
        fit[at, :] = first.T
        sit[at, :] = second.T
        cot[at, :] = cotan.T

    def mm(a, b):
        return jnp.dot(a, b, preferred_element_type=f32)

    def mm_cols(a, b):
        return lax.dot_general(a, b, (((1,), (1,)), ((), ())), preferred_element_type=f32)

    def mm_rows(a, b):
        return lax.dot_general(a, b, (((0,), (0,)), ((), ())), preferred_element_type=f32)

    seg_row = seg_ref[pl.ds(row, 1), :].astype(f32)
    seg_col = jnp.broadcast_to(seg_row, (8, length)).T[:, 0:1]
    spans = []
    pos = []
    for i in range(length // QBLOCK):
        lo = max(0, i * QBLOCK - WINDOW)
        hi = (i + 1) * QBLOCK
        spans.append((i * QBLOCK, lo, hi))
    masks = []
    for at, lo, hi in spans:
        shape = (QBLOCK, hi - lo)
        qi = lax.broadcasted_iota(jnp.int32, shape, 0) + at
        ki = lax.broadcasted_iota(jnp.int32, shape, 1) + lo
        allowed = (seg_col[at:hi] == seg_row[:, lo:hi]) & (ki <= qi)
        masks.append(allowed)
        pos.append(jnp.sum(jnp.where(allowed, 1.0, 0.0), 1, keepdims=True) - 1.0)
    angle = jnp.concatenate(pos, 0) * freq_ref[0:1, :]
    cosine = jnp.cos(angle)
    sine = jnp.sin(angle)
    lane = lax.rem(lax.broadcasted_iota(jnp.int32, (length, LANES), 1), HEAD_DIM)
    half = ROT_DIM // 2
    up = jnp.where(lane < half, -sine, 0.0)
    down = jnp.where((lane >= half) & (lane < ROT_DIM), sine, 0.0)

    def turn(tile, sign):
        return (tile * cosine + sign * (pltpu.roll(tile, LANES - half, 1) * up
                                        + pltpu.roll(tile, half, 1) * down))

    landed(0)
    landed(2)
    dcat[...] = mm(co[...], wo[:, :attn]).astype(bf16)
    lowq = lane_low((length, LANES))
    lowb = lane_low((QBLOCK, LANES))
    scale = 1.0 / math.sqrt(HEAD_DIM)

    def pair_step(p, carry):
        at = pl.multiple_of(p * 3 * LANES, 3 * LANES)
        out_at = pl.ds(pl.multiple_of(p * LANES, LANES), LANES)
        packed = mm(fi[...], wq[:, pl.ds(at, 3 * LANES)])
        t0, t1, t2 = (packed[:, n * LANES:(n + 1) * LANES] for n in range(3))
        query = turn(jnp.where(lowq, t0, t1), 1.0).astype(bf16)
        keys = turn(swap(jnp.where(lowq, t2, t0)), 1.0).astype(bf16)
        values = jnp.where(lowq, t1, t2).astype(bf16)
        grads = dcat[:, out_at]
        dk[...] = jnp.zeros_like(dk)
        dv[...] = jnp.zeros_like(dv)
        zero = jnp.zeros((), bf16)
        dqs = []
        for (at_q, lo, hi), allowed in zip(spans, masks):
            qb = query[at_q:hi]
            gb = grads[at_q:hi]
            kw, vw = keys[lo:hi], values[lo:hi]
            mixed, dq, keep = [], [], []
            for head in range(2):
                sel = lowb if head == 0 else jnp.logical_not(lowb)
                qm = jnp.where(sel, qb, zero)
                gm = jnp.where(sel, gb, zero)
                scores = jnp.where(allowed, mm_cols(qm, kw) * scale, mask_fill)
                logsum = jnp.log(jnp.sum(jnp.exp(scores), 1, keepdims=True))
                probs = jnp.exp(scores - logsum)
                weights = probs.astype(bf16)
                got = mm(weights, vw).astype(bf16)
                delta = jnp.sum(gm.astype(f32) * got.astype(f32), 1, keepdims=True)
                prod = mm_cols(gm, vw)
                score_grad = (probs * (prod - delta) * scale).astype(bf16)
                mixed.append(got)
                dq.append(mm(score_grad, kw))
                dk[lo:hi, :] += mm_rows(score_grad, qm)
                dv[lo:hi, :] += mm_rows(weights, gm)
            act[at_q:hi, out_at] = jnp.where(lowb, mixed[0], mixed[1])
            dqs.append(jnp.where(lowb, dq[0], dq[1]))
        dquery = turn(jnp.concatenate(dqs, 0), -1.0)
        dkeys = swap(turn(dk[...], -1.0))
        dvals = dv[...]
        pg[:, pl.ds(at, LANES)] = jnp.where(lowq, dquery, dkeys).astype(bf16)
        pg[:, pl.ds(pl.multiple_of(at + LANES, LANES), LANES)] = jnp.where(
            lowq, dvals, dquery).astype(bf16)
        pg[:, pl.ds(pl.multiple_of(at + 2 * LANES, LANES), LANES)] = jnp.where(
            lowq, dkeys, dvals).astype(bf16)
        return carry

    lax.fori_loop(0, attn // LANES, pair_step, 0)

    landed(1)
    step = 2 * LANES

    def hidden_step(n, carry):
        at = pl.ds(pl.multiple_of(n * step, step), step)
        at_out = pl.ds(pl.multiple_of(attn + n * step, LANES), step)
        value = mm(si[...], wu[:, at])
        erf = 0.5 * (1.0 + lax.erf(value * inv_sqrt_two))
        act[:, at_out] = (value * erf).astype(bf16)
        slope = erf + value * inv_sqrt_two_pi * jnp.exp(-0.5 * value * value)
        hg[:, at] = (mm(co[...], wo[:, at_out]) * slope).astype(bf16)
        return carry

    lax.fori_loop(0, hidden // step, hidden_step, 0)

    def spread_rows(ref, at, value):
        value = value.astype(bf16)
        for r in range(row_count):
            ref[r, :LANES, at] = value[r * LANES:(r + 1) * LANES]
            ref[r, LANES:, at] = value[tail + r * small:tail + (r + 1) * small]

    def weight_grads(ref, left, right, size):
        count = size // step

        def one(n, carry):
            at = pl.ds(pl.multiple_of(n * step, step), step)
            spread_rows(ref, at, mm(left[...], right[:, at]))
            return carry

        lax.fori_loop(0, count, one, 0)
        if size % step:
            at = slice(count * step, size)
            spread_rows(ref, at, mm(left[...], right[:, at]))

    weight_grads(go, cot, act, act.shape[1])
    weight_grads(gu, sit, hg, hidden)
    weight_grads(gq, fit, pg, pg.shape[1])

    def put_tiles(ref, chunks):
        for r in range(row_count):
            ref[r, :length, :] = chunks[r].astype(bf16)
        for p in range(row_count // 2):
            both = chunks[row_count + p]
            top, bottom = both[:halflen], both[halflen:]
            ref[2 * p, length:, :] = jnp.where(low, top, swap(bottom)).astype(bf16)
            ref[2 * p + 1, length:, :] = jnp.where(low, swap(top), bottom).astype(bf16)

    def split(value):
        return [value[:, n * LANES:(n + 1) * LANES] for n in range(value.shape[1] // LANES)]

    out_tiles, back1, back2 = [], 0.0, 0.0
    sums = []
    for n in range(width // step):
        at = slice(n * step, (n + 1) * step)
        out_tiles += split(mm_cols(act[...], wo[at, :]))
        first = mm_cols(pg[...], wq[at, :])
        second = mm_cols(hg[...], wu[at, :])
        value = normed[:, at]
        gains = jnp.concatenate([norm_tile(2 * n), norm_tile(2 * n + 1)], 1)
        four = jnp.concatenate(
            [jnp.sum(first * value, 0, keepdims=True), jnp.sum(first, 0, keepdims=True),
             jnp.sum(second * value, 0, keepdims=True), jnp.sum(second, 0, keepdims=True),
             jnp.zeros((4, step), f32)], 0)
        sums += split(four)
        both = gains[0:1] * first + gains[2:3] * second
        comb[:, at] = both
        back1 = back1 + jnp.sum(both, 1, keepdims=True)
        back2 = back2 + jnp.sum(both * value, 1, keepdims=True)
    put_tiles(outp, out_tiles)
    grad_tiles = []
    for n in range(width // LANES):
        at = slice(n * LANES, (n + 1) * LANES)
        grad_tiles.append(
            rstd * (comb[:, at] - back1 / width - normed[:, at] * (back2 / width)))
    put_tiles(gradp, grad_tiles)
    for r in range(row_count):
        nrmp[r, :, :LANES] = sums[r]
    for p in range(row_count // 2):
        both = sums[row_count + p]
        nrmp[2 * p, :, LANES:] = both
        nrmp[2 * p + 1, :, LANES:] = swap(both)


def compute_all(row_count, width, segs, freq, xg, cg, ng, own, gathered):
    bf16, f32 = jnp.bfloat16, jnp.float32
    length = segs.shape[1]
    n = row_count
    vmem = pl.BlockSpec(memory_space=pltpu.VMEM)
    anywhere = pl.BlockSpec(memory_space=pl.ANY)
    sizes = [w.shape[1] for w in own]
    local = own[0].shape[0]
    return pl.pallas_call(
        functools.partial(compute_kernel, n, width),
        out_shape=[
            jax.ShapeDtypeStruct(xg.shape, bf16),
            jax.ShapeDtypeStruct(xg.shape, bf16),
            jax.ShapeDtypeStruct(ng.shape, f32),
        ] + [jax.ShapeDtypeStruct((n, local, s), bf16) for s in sizes],
        in_specs=[vmem] * 5 + [anywhere] * 6,
        out_specs=[vmem] * 6,
        scratch_shapes=[pltpu.VMEM((width, s), bf16) for s in sizes] + [
            pltpu.VMEM((length, width), f32),
            pltpu.VMEM((length, width), bf16),
            pltpu.VMEM((length, width), bf16),
            pltpu.VMEM((length, width), bf16),
            pltpu.VMEM((width, length), bf16),
            pltpu.VMEM((width, length), bf16),
            pltpu.VMEM((width, length), bf16),
            pltpu.VMEM((length, sizes[0] // 3), bf16),
            pltpu.VMEM((length, sizes[2]), bf16),
            pltpu.VMEM((length, sizes[1]), bf16),
            pltpu.VMEM((length, sizes[0]), bf16),
            pltpu.VMEM((length, width), f32),
            pltpu.VMEM((length, LANES), f32),
            pltpu.VMEM((length, LANES), f32),
            pltpu.SemaphoreType.DMA((2, 3, n)),
        ],
        compiler_params=pltpu.CompilerParams(vmem_limit_bytes=56 << 20),
        name="compute",
    )(segs, freq, xg, cg, ng, *own, *gathered)


def pack_tokens(rows, length):
    blocks = rows.reshape(-1, length, rows.shape[1])
    ends = blocks[:, :, LANES:]
    joined = jnp.concatenate([ends[:, :length // 2], ends[:, length // 2:]], 2)
    return jnp.concatenate([blocks[:, :, :LANES], joined], 1)


def unpack_tokens(blocks, length):
    joined = blocks[:, length:]
    small = joined.shape[2] // 2
    ends = jnp.concatenate([joined[:, :, :small], joined[:, :, small:]], 1)
    return jnp.concatenate([blocks[:, :length], ends], 2).reshape(-1, LANES + small)


def on_device(
    tokens_in,
    out_cot,
    segments,
    norm_params,
    qkv_weight,
    proj_weight,
    up_weight,
    down_weight,
    norm_first,
    norm_second,
    qkv_first,
    qkv_second,
    proj_first,
    proj_second,
    up_first,
    up_second,
    down_first,
    down_second,
):
    row_count = lax.axis_size("row")
    data_count = lax.axis_size("dp")
    col_count = lax.axis_size("col")
    local_count, local_width = tokens_in.shape
    width = local_width * row_count
    length = segments.shape[1]
    shares = local_count // length
    bf16 = jnp.bfloat16

    proj_t, down_t = proj_weight.T, down_weight.T
    own = (
        qkv_weight.astype(bf16),
        up_weight.astype(bf16),
        jnp.concatenate([proj_t.astype(bf16), down_t.astype(bf16)], 1),
    )
    nrm = jnp.pad(norm_params, ((0, 4), (0, 2 * LANES - local_width)))
    xg, cg, ng, *gathered = gather_all(
        row_count, pack_tokens(tokens_in, length), pack_tokens(out_cot, length), nrm, own)

    half = ROT_DIM // 2
    freq = rotary_base ** (-2.0 * jnp.arange(half, dtype=jnp.float32) / ROT_DIM)
    freq = jnp.concatenate([freq, freq, jnp.zeros(HEAD_DIM - ROT_DIM, jnp.float32)])
    freq = jnp.broadcast_to(jnp.tile(freq, 2)[None], (8, LANES))
    outp, gradp, nrmp, *parts = compute_all(
        row_count, width, segments, freq, xg, cg, ng, own, gathered)
    out_sum, grad_sum, norm_sum, qkv_sum, up_sum, out_w = reduce_all(
        row_count, data_count, shares, outp, gradp, nrmp, parts)

    output = (tokens_in.astype(jnp.float32)
              + unpack_tokens(out_sum, length).astype(jnp.float32)).astype(bf16)
    input_grad = (out_cot.astype(jnp.float32)
                  + unpack_tokens(grad_sum, length).astype(jnp.float32)).astype(bf16)
    norm_grad = norm_sum[:4, :local_width]
    qkv_grad = qkv_sum.astype(jnp.float32)
    up_grad = up_sum.astype(jnp.float32)
    attn_width = proj_weight.shape[0]
    proj_grad = out_w[:, :attn_width].astype(jnp.float32).T
    down_grad = out_w[:, attn_width:].astype(jnp.float32).T
    norm_new, norm_first_new, norm_second_new = adam_update(
        norm_params, norm_first, norm_second, norm_grad, 0.0
    )
    qkv_new, qkv_first_new, qkv_second_new = adam_update(
        qkv_weight, qkv_first, qkv_second, qkv_grad, decay_rate
    )
    proj_new, proj_first_new, proj_second_new = adam_update(
        proj_weight, proj_first, proj_second, proj_grad, decay_rate
    )
    up_new, up_first_new, up_second_new = adam_update(
        up_weight, up_first, up_second, up_grad, decay_rate
    )
    down_new, down_first_new, down_second_new = adam_update(
        down_weight, down_first, down_second, down_grad, decay_rate
    )
    return (
        output,
        input_grad,
        norm_grad,
        qkv_grad,
        proj_grad,
        up_grad,
        down_grad,
        norm_new,
        qkv_new,
        proj_new,
        up_new,
        down_new,
        norm_first_new,
        norm_second_new,
        qkv_first_new,
        qkv_second_new,
        proj_first_new,
        proj_second_new,
        up_first_new,
        up_second_new,
        down_first_new,
        down_second_new,
    )


def solution(mesh):
    placed = (
        P(("dp", "col"), "row"),
        P(("dp", "col"), "row"),
        P("dp", None),
        P(None, "row"),
        P("row", "col"),
        P("col", "row"),
        P("row", "col"),
        P("col", "row"),
        P(None, "row"),
        P(None, "row"),
        P("row", "col"),
        P("row", "col"),
        P("col", "row"),
        P("col", "row"),
        P("row", "col"),
        P("row", "col"),
        P("col", "row"),
        P("col", "row"),
    )
    return jax.shard_map(
        on_device,
        mesh=mesh,
        in_specs=placed,
        out_specs=(
            P(("dp", "col"), "row"),
            P(("dp", "col"), "row"),
            P(None, "row"),
            P("row", "col"),
            P("col", "row"),
            P("row", "col"),
            P("col", "row"),
            P(None, "row"),
            P("row", "col"),
            P("col", "row"),
            P("row", "col"),
            P("col", "row"),
            P(None, "row"),
            P(None, "row"),
            P("row", "col"),
            P("row", "col"),
            P("col", "row"),
            P("col", "row"),
            P("row", "col"),
            P("row", "col"),
            P("col", "row"),
            P("col", "row"),
        ),
        check_vma=False,
    )
```

```python
import functools
import math
import types

import jax
import jax.numpy as jnp
from jax import lax
from jax.experimental import pallas as pl
from jax.experimental.pallas import tpu as pltpu
from jax.sharding import PartitionSpec as P

D = 768
HEAD_DIM = 64
ROT_DIM = 16
SEQ_LEN = 512
STEP = 3


norm_eps = 1e-05
rotary_base = 10000.0
learn_rate = 0.01
beta_first = 0.9
beta_second = 0.95
adam_eps = 1e-08
decay_rate = 0.1
mask_fill = -1e30
inv_sqrt_two = 0.7071067811865476
inv_sqrt_two_pi = 0.3989422804014327


def adam_update(weight, first, second, grad, decay):
    first_new = beta_first * first + (1.0 - beta_first) * grad
    second_new = beta_second * second + (1.0 - beta_second) * grad * grad
    first_hat = first_new / (1.0 - beta_first**STEP)
    second_hat = second_new / (1.0 - beta_second**STEP)
    weight_new = weight - learn_rate * (
        first_hat / (jnp.sqrt(second_hat) + adam_eps) + decay * weight
    )
    return (weight_new, first_new, second_new)


MESH = pl.DeviceIdType.MESH
LANES = 128
QUARTERS = 4
WINDOW = 256
QBLOCK = 128


def remote(src, dst, send_sem, recv_sem, device):
    return pltpu.make_async_remote_copy(
        src_ref=src,
        dst_ref=dst,
        send_sem=send_sem,
        recv_sem=recv_sem,
        device_id=device,
        device_id_type=MESH,
    )


def places(row_count):
    data, row, col = lax.axis_index("dp"), lax.axis_index("row"), lax.axis_index("col")
    quarter = lax.rem(data, QUARTERS)
    far = data - quarter + lax.rem(quarter + 2, QUARTERS)
    mate = data + 1 - 2 * lax.rem(quarter, 2)
    return data, row, col, quarter, far, mate


def greet(peers):
    barrier = pltpu.get_barrier_semaphore()
    for peer in peers:
        pl.semaphore_signal(barrier, inc=1, device_id=peer, device_id_type=MESH)
    pl.semaphore_wait(barrier, len(peers))


def gatherer(row_count, at, tok, cot, nrm, own_w, all_w, s):
    data, row, col, quarter, far, mate = at
    shares = tok.shape[0]
    other = 1 - col
    home = lax.div(row, shares)
    groups = len(own_w)
    local = own_w[0].shape[0]
    depth = local // QUARTERS
    others = [lax.rem(row + k, row_count) for k in range(1, row_count)]

    def rows(src, part):
        return pl.ds(pl.multiple_of(src * local + part * depth, depth), depth)

    def step_copy(g, src, up):
        ref = all_w[g].at[rows(src, quarter)]
        return remote(ref, ref, s.z_s.at[int(up), g, src], s.z_r.at[g, src],
                      (data, row + 1 if up else row - 1, col))

    def own_copy(g, up):
        return remote(own_w[g].at[rows(0, quarter)], all_w[g].at[rows(row, quarter)],
                      s.z_s.at[int(up), g, row], s.z_r.at[g, row],
                      (data, row + 1 if up else row - 1, col))

    def own_local(g):
        dest = all_w[g].at[pl.ds(pl.multiple_of(row * local, local), local)]
        return pltpu.make_async_copy(own_w[g], dest, s.own_l.at[g])

    def far_copy(g, src):
        ref = all_w[g].at[rows(src, quarter)]
        return remote(ref, ref, s.f_s.at[g, src], s.f_r.at[g, src], (far, row, col))

    def far_wait(g, src):
        ref = all_w[g].at[rows(src, lax.rem(quarter + 2, QUARTERS))]
        remote(ref, ref, s.f_s.at[g, src], s.f_r.at[g, src], (far, row, col)).wait_recv()

    def mate_copy(g, src, second):
        part = lax.rem(quarter + 2, QUARTERS) if second else quarter
        ref = all_w[g].at[rows(src, part)]
        return remote(ref, ref, s.m_s.at[int(second), g, src], s.m_r.at[int(second), g, src],
                      (mate, row, col))

    def mate_wait(g, src, second):
        theirs = quarter + 1 - 2 * lax.rem(quarter, 2)
        part = lax.rem(theirs + 2, QUARTERS) if second else theirs
        ref = all_w[g].at[rows(src, part)]
        remote(ref, ref, s.m_s.at[int(second), g, src], s.m_r.at[int(second), g, src],
               (mate, row, col)).wait_recv()

    def norm_copy(k):
        return remote(nrm, s.ng.at[row], s.nrm_s.at[k], s.nrm_r.at[row], (data, others[k], col))

    def norm_wait(k):
        remote(nrm, s.ng.at[others[k]], s.nrm_s.at[k], s.nrm_r.at[others[k]],
               (data, others[k], col)).wait_recv()

    def norm_local():
        return pltpu.make_async_copy(nrm, s.ng.at[row], s.loc.at[2])

    def token_copy(j):
        return remote(tok.at[j], s.xg.at[row], s.x_s.at[j], s.x_r.at[row],
                      (data, col * shares + j, col))

    def token_local(j):
        return pltpu.make_async_copy(tok.at[j], s.xg.at[row], s.loc.at[0])

    def hop_copy(j):
        return remote(cot.at[j], s.hop.at[j], s.h_s.at[j], s.h_r.at[j], (data, row, other))

    def cot_copy(j):
        return remote(s.hop.at[j], s.cg.at[row], s.c_s.at[j], s.c_r.at[row],
                      (data, other * shares + j, col))

    def cot_local(j):
        return pltpu.make_async_copy(s.hop.at[j], s.cg.at[row], s.loc.at[1])

    def x_wait(src):
        remote(tok.at[0], s.xg.at[src], s.x_s.at[0], s.x_r.at[src],
               (data, src, col)).wait_recv()

    def c_wait(src):
        remote(tok.at[0], s.cg.at[src], s.c_s.at[0], s.c_r.at[src],
               (data, src, col)).wait_recv()

    def across(which, src):
        ref, send, recv = ((s.xg, s.xy_s, s.xy_r), (s.cg, s.cy_s, s.cy_r))[which]
        return remote(ref.at[src], ref.at[src], send.at[src], recv.at[src],
                      (data, row, other))

    mains = (col == home, col != home)

    def begin():
        for k in range(row_count - 1):
            norm_copy(k).start()
        norm_local().start()
        for j in range(shares):
            @pl.when(col * shares + j != row)
            def _():
                token_copy(j).start()

            @pl.when(col * shares + j == row)
            def _():
                token_local(j).start()
            hop_copy(j).start()
        for g in range(groups):
            own_local(g).start()

    def send_own(g):
        @pl.when(row + 1 < row_count)
        def _():
            own_copy(g, True).start()

        @pl.when(row > 0)
        def _():
            own_copy(g, False).start()

    def cot_hop():
        for j in range(shares):
            hop_copy(j).wait_recv()

            @pl.when(other * shares + j != row)
            def _():
                cot_copy(j).start()

            @pl.when(other * shares + j == row)
            def _():
                cot_local(j).start()

    def forward(which):
        @pl.when(mains[which])
        def _():
            (token_local, cot_local)[which](0).wait()
            across(which, row).start()
            for src in others:
                (x_wait, c_wait)[which](src)
                across(which, src).start()

    def arrived(which):
        @pl.when(jnp.logical_not(mains[which]))
        def _():
            for src in range(row_count):
                across(which, src).wait_recv()

    def norm_arrived():
        norm_local().wait()
        for k in range(row_count - 1):
            norm_wait(k)

    pending = []

    def settle():
        for g, k, below in pending:
            src = row - k if below else row + k

            @pl.when(src >= 0 if below else src < row_count)
            def _():
                far_wait(g, src)
                mate_copy(g, src, True).start()
        pending.clear()

    def relay(g, k):
        now = []
        for below in (True, False):
            src = row - k if below else row + k

            @pl.when(src >= 0 if below else src < row_count)
            def _():
                step_copy(g, src, below).wait_recv()
                onward = row + 1 < row_count if below else row > 0

                @pl.when(onward)
                def _():
                    step_copy(g, src, below).start()
                far_copy(g, src).start()
                mate_copy(g, src, False).start()
            now.append((g, k, below))
        settle()
        pending.extend(now)

    def landed(g):
        own_local(g).wait()
        for k in range(1, row_count):
            for second in (False, True):
                mate_wait(g, others[k - 1], second)

    def drain():
        for which in range(2):
            @pl.when(mains[which])
            def _():
                for src in range(row_count):
                    across(which, src).wait_send()
        for k in range(row_count - 1):
            norm_copy(k).wait_send()
        for j in range(shares):
            @pl.when(col * shares + j != row)
            def _():
                token_copy(j).wait_send()

            @pl.when(other * shares + j != row)
            def _():
                cot_copy(j).wait_send()
            hop_copy(j).wait_send()
        for g in range(groups):
            @pl.when(row + 1 < row_count)
            def _():
                own_copy(g, True).wait_send()

            @pl.when(row > 0)
            def _():
                own_copy(g, False).wait_send()
            for k in range(1, row_count):
                for below in (True, False):
                    src = row - k if below else row + k

                    @pl.when(src >= 0 if below else src < row_count)
                    def _():
                        onward = row + 1 < row_count if below else row > 0

                        @pl.when(onward)
                        def _():
                            step_copy(g, src, below).wait_send()
                        far_copy(g, src).wait_send()
                        for second in (False, True):
                            mate_copy(g, src, second).wait_send()

    return types.SimpleNamespace(
        begin=begin, send_own=send_own, cot_hop=cot_hop, forward=forward, arrived=arrived,
        norm_arrived=norm_arrived, settle=settle, relay=relay, landed=landed, drain=drain)


def reducer(row_count, groups_out, at, parts, total, out_t, grad_t, nrm_t, s):
    data, row, col, quarter, far, mate = at
    groups = len(parts)
    shares = out_t.shape[0]
    other = 1 - col
    home = lax.div(row, shares)
    local = parts[0].shape[0] // row_count
    depth = local // QUARTERS
    data_count = QUARTERS * groups_out
    block = lax.div(data, QUARTERS)
    others = [lax.rem(row + k, row_count) for k in range(1, row_count)]
    order = others + [row]
    wider = [lax.rem(data + QUARTERS * k, data_count) for k in range(1, groups_out)]
    everyone = [lax.rem(data + k, data_count) for k in range(1, data_count)]
    f32, bf16 = jnp.float32, jnp.bfloat16
    half = lax.rem(quarter + 2, QUARTERS)
    theirs = quarter + 1 - 2 * lax.rem(quarter, 2)
    theirs_half = lax.rem(theirs + 2, QUARTERS)
    slot = row - home * shares

    def rows(t, part):
        return pl.ds(pl.multiple_of(t * local + part * depth, depth), depth)

    def norm_z(k):
        return remote(s.nrmp.at[others[k]], s.nz.at[row], s.nz_s.at[k], s.nz_r.at[row],
                      (data, others[k], col))

    def norm_z_wait(k):
        remote(s.nrmp.at[0], s.nz.at[others[k]], s.nz_s.at[k], s.nz_r.at[others[k]],
               (data, others[k], col)).wait_recv()

    def norm_c():
        return remote(s.nrm1, s.nc, s.nc_s.at[0], s.nc_r.at[0], (data, row, other))

    def norm_d(k):
        return remote(s.nrm2, s.nd.at[data], s.nd_s.at[k], s.nd_r.at[data],
                      (everyone[k], row, col))

    def norm_d_wait(k):
        remote(s.nrm2, s.nd.at[everyone[k]], s.nd_s.at[k], s.nd_r.at[everyone[k]],
               (everyone[k], row, col)).wait_recv()

    def out_y(t):
        return remote(s.outp.at[t], s.oy.at[t], s.oy_s.at[t], s.oy_r.at[t], (data, row, other))

    def grad_y(t):
        return remote(s.gradp.at[t], s.gy.at[t], s.gy_s.at[t], s.gy_r.at[t],
                      (data, row, other))

    def out_z(t):
        return remote(s.od.at[t], out_t.at[slot], s.oz_s.at[t], s.oz_r.at[slot],
                      (data, t, col))

    def out_local():
        return pltpu.make_async_copy(s.od.at[row], out_t.at[slot], s.loc.at[3])

    def out_z_wait(j):
        remote(s.od.at[0], out_t.at[j], s.oz_s.at[0], s.oz_r.at[j],
               (data, row, col)).wait_recv()

    def grad_z(t):
        return remote(s.gd.at[t], s.gh.at[slot], s.gz_s.at[t], s.gz_r.at[slot],
                      (data, t, col))

    def grad_local():
        return pltpu.make_async_copy(s.gd.at[row], s.gh.at[slot], s.loc.at[4])

    def grad_z_wait(j):
        remote(s.gd.at[0], s.gh.at[j], s.gz_s.at[0], s.gz_r.at[j],
               (data, row, col)).wait_recv()

    def grad_h(j):
        return remote(s.gh.at[j], grad_t.at[j], s.gh_s.at[j], s.gh_r.at[j], (data, row, other))

    def mate_part(g, t, second):
        part = theirs_half if second else theirs
        return remote(parts[g].at[rows(t, part)], s.crecv[g].at[int(second), t],
                      s.pc_s.at[int(second), g, t], s.pc_r.at[int(second), g, t],
                      (mate, row, col))

    def far_part(g, t):
        return remote(s.fsend[g].at[t], s.frecv[g].at[t], s.pf_s.at[g, t], s.pf_r.at[g, t],
                      (far, row, col))

    def row_part(g, t):
        return remote(s.zsend[g].at[t], s.zrecv[g].at[row], s.pz_s.at[g, t], s.pz_r.at[g, row],
                      (data, t, col))

    def row_wait(g, src):
        remote(s.zsend[g].at[src], s.zrecv[g].at[src], s.pz_s.at[g, src], s.pz_r.at[g, src],
               (data, src, col)).wait_recv()

    def wide_part(g, k):
        return remote(total[g].at[rows(0, quarter)], s.extra[g].at[block],
                      s.e_s.at[g, k], s.e_r.at[g, block], (wider[k], row, col))

    def wide_wait(g, k):
        src = lax.div(wider[k], QUARTERS)
        remote(total[g].at[rows(0, quarter)], s.extra[g].at[src],
               s.e_s.at[g, k], s.e_r.at[g, src], (wider[k], row, col)).wait_recv()

    def far_sum(g):
        ref = total[g].at[rows(0, quarter)]
        return remote(ref, ref, s.a_s.at[g], s.a_r.at[g], (far, row, col))

    def far_sum_wait(g):
        ref = total[g].at[rows(0, half)]
        remote(ref, ref, s.a_s.at[g], s.a_r.at[g], (far, row, col)).wait_recv()

    def mate_sum(g, second):
        ref = total[g].at[rows(0, half if second else quarter)]
        return remote(ref, ref, s.b_s.at[int(second), g], s.b_r.at[int(second), g],
                      (mate, row, col))

    def mate_sum_wait(g, second):
        ref = total[g].at[rows(0, theirs_half if second else theirs)]
        remote(ref, ref, s.b_s.at[int(second), g], s.b_r.at[int(second), g],
               (mate, row, col)).wait_recv()

    o_main = col == home
    g_main = col != home

    def start(g):
        for t in order:
            mate_part(g, t, True).start()
        for t in order:
            mate_part(g, t, False).start()

    def start_out():
        @pl.when(jnp.logical_not(o_main))
        def _():
            for t in order:
                out_y(t).start()

    def start_grad():
        @pl.when(jnp.logical_not(g_main))
        def _():
            for t in order:
                grad_y(t).start()

    def start_norm():
        for k in range(row_count - 1):
            norm_z(k).start()

    def stage_far(g, t):
        mate_part(g, t, True).wait_recv()
        own = parts[g][rows(t, half), :].astype(f32)
        s.fsend[g][t] = (own + s.crecv[g][1, t].astype(f32)).astype(bf16)
        far_part(g, t).start()

    def stage_row(g, t):
        mate_part(g, t, False).wait_recv()
        far_part(g, t).wait_recv()
        mine = parts[g][rows(t, quarter), :].astype(f32)
        mine = mine + s.crecv[g][0, t].astype(f32) + s.frecv[g][t].astype(f32)
        s.zsend[g][t] = mine.astype(bf16)
        if t is not row:
            row_part(g, t).start()

    def outputs_out():
        @pl.when(o_main)
        def _():
            for t in order:
                out_y(t).wait_recv()
                s.od[t] = (s.outp[t].astype(f32) + s.oy[t].astype(f32)).astype(bf16)
                if t is row:
                    out_local().start()
                else:
                    out_z(t).start()

    def outputs_grad():
        @pl.when(g_main)
        def _():
            for t in order:
                grad_y(t).wait_recv()
                s.gd[t] = (s.gradp[t].astype(f32) + s.gy[t].astype(f32)).astype(bf16)
                if t is row:
                    grad_local().start()
                else:
                    grad_z(t).start()

    def grads_home():
        for j in range(shares):
            @pl.when(other * shares + j != row)
            def _():
                grad_z_wait(j)

            @pl.when(other * shares + j == row)
            def _():
                grad_local().wait()
            grad_h(j).start()

    def norm_rows():
        acc = s.nrmp[row]
        for k in range(row_count - 1):
            norm_z_wait(k)
            acc = acc + s.nz[others[k]]
        s.nrm1[...] = acc
        norm_c().start()

    def norm_cols():
        norm_c().wait_recv()
        s.nrm2[...] = s.nrm1[...] + s.nc[...]
        for k in range(len(everyone)):
            norm_d(k).start()

    def norm_last():
        acc = s.nrm2[...]
        for k in range(len(everyone)):
            norm_d_wait(k)
            acc = acc + s.nd[everyone[k]]
        nrm_t[...] = acc

    def finish(g):
        acc = s.zsend[g][row].astype(f32)
        for src in others:
            row_wait(g, src)
            acc = acc + s.zrecv[g][src].astype(f32)
        total[g][rows(0, quarter), :] = acc.astype(bf16)
        if wider:
            for k in range(len(wider)):
                wide_part(g, k).start()
            for k in range(len(wider)):
                wide_wait(g, k)
                acc = acc + s.extra[g][lax.div(wider[k], QUARTERS)].astype(f32)
            for k in range(len(wider)):
                wide_part(g, k).wait_send()
            total[g][rows(0, quarter), :] = acc.astype(bf16)
        far_sum(g).start()
        mate_sum(g, False).start()

    def spread(g):
        far_sum_wait(g)
        mate_sum(g, True).start()

    def drain():
        @pl.when(jnp.logical_not(o_main))
        def _():
            for t in range(row_count):
                out_y(t).wait_send()

        @pl.when(jnp.logical_not(g_main))
        def _():
            for t in range(row_count):
                grad_y(t).wait_send()

        @pl.when(o_main)
        def _():
            out_local().wait()
            for t in others:
                out_z(t).wait_send()

        @pl.when(g_main)
        def _():
            for t in others:
                grad_z(t).wait_send()
        for j in range(shares):
            @pl.when(col * shares + j != row)
            def _():
                out_z_wait(j)
            grad_h(j).wait()
        for k in range(row_count - 1):
            norm_z(k).wait_send()
        norm_c().wait_send()
        for k in range(len(everyone)):
            norm_d(k).wait_send()
        for g in range(groups):
            for t in range(row_count):
                for second in (False, True):
                    mate_part(g, t, second).wait_send()
                far_part(g, t).wait_send()
            for t in others:
                row_part(g, t).wait_send()
            far_sum(g).wait_send()
            for second in (False, True):
                mate_sum(g, second).wait_send()
                mate_sum_wait(g, second)

    return types.SimpleNamespace(
        order=order, everyone=everyone, start=start, start_out=start_out, start_grad=start_grad,
        start_norm=start_norm, stage_far=stage_far, stage_row=stage_row,
        outputs_out=outputs_out, outputs_grad=outputs_grad, grads_home=grads_home,
        norm_rows=norm_rows, norm_cols=norm_cols, norm_last=norm_last, finish=finish,
        spread=spread, drain=drain)


def lane_low(shape):
    return lax.broadcasted_iota(jnp.int32, shape, len(shape) - 1) < HEAD_DIM


def swap(tile):
    return pltpu.roll(tile, HEAD_DIM, 1)


def layer_kernel(row_count, width, groups_out, names, tok, cotan, nrm, seg_ref, freq_ref,
                 w0, w1, w2, w3, out_t, grad_t, nrm_t, r0, r1, r2, r3, *scratch):
    s = types.SimpleNamespace()
    for name, ref in zip(names, scratch):
        if name[-1].isdigit() and name[:-1] in LISTS:
            vars(s).setdefault(name[:-1], []).append(ref)
        else:
            setattr(s, name, ref)
    f32, bf16 = jnp.float32, jnp.bfloat16
    at = places(row_count)
    data, row, col, quarter, far, mate = at
    gat = gatherer(row_count, at, tok, cotan, nrm, (w0, w1, w2, w3), s.whole, s)
    red = reducer(row_count, groups_out, at, s.part, (r0, r1, r2, r3), out_t, grad_t, nrm_t, s)
    wq, wp, wd, wu = s.whole
    gq, gp, gd, gu = s.part
    length = s.xg.shape[1] * 2 // 3
    halflen = length // 2
    attn = wp.shape[1]
    hidden = wu.shape[1]
    last = row_count - 1

    greet([(data, lax.rem(row + k, row_count), col) for k in range(1, row_count)]
          + [(data, row, 1 - col)] + [(t, row, col) for t in red.everyone])

    def mm(a, b):
        return jnp.dot(a, b, preferred_element_type=f32)

    def mm_cols(a, b):
        return lax.dot_general(a, b, (((1,), (1,)), ((), ())), preferred_element_type=f32)

    def mm_rows(a, b):
        return lax.dot_general(a, b, (((0,), (0,)), ((), ())), preferred_element_type=f32)

    gat.begin()
    gat.send_own(0)
    gat.send_own(1)

    seg_row = seg_ref[pl.ds(row, 1), :].astype(f32)
    seg_col = jnp.broadcast_to(seg_row, (8, length)).T[:, 0:1]
    spans, pos = [], []
    for i in range(length // QBLOCK):
        spans.append((i * QBLOCK, max(0, i * QBLOCK - WINDOW), (i + 1) * QBLOCK))
    for n, (start, lo, hi) in enumerate(spans):
        shape = (QBLOCK, hi - lo)
        qi = lax.broadcasted_iota(jnp.int32, shape, 0) + start
        ki = lax.broadcasted_iota(jnp.int32, shape, 1) + lo
        allowed = (seg_col[start:hi] == seg_row[:, lo:hi]) & (ki <= qi)
        seen = jnp.where(allowed, 1.0, 0.0)
        s.mask[n, :, :hi - lo] = seen
        pos.append(jnp.sum(seen, 1, keepdims=True) - 1.0)
    angle = jnp.concatenate(pos, 0) * freq_ref[0:1, :]
    s.cosine[...] = jnp.cos(angle)
    s.sine[...] = jnp.sin(angle)
    lane = lax.rem(lax.broadcasted_iota(jnp.int32, (length, LANES), 1), HEAD_DIM)
    half = ROT_DIM // 2

    def turn(tile, sign):
        sine = s.sine[...]
        up = jnp.where(lane < half, -sine, 0.0)
        down = jnp.where((lane >= half) & (lane < ROT_DIM), sine, 0.0)
        return (tile * s.cosine[...] + sign * (pltpu.roll(tile, LANES - half, 1) * up
                                               + pltpu.roll(tile, half, 1) * down))

    gat.forward(0)
    gat.cot_hop()
    gat.relay(0, 1)
    gat.send_own(2)
    for k in range(2, row_count):
        gat.relay(0, k)
    gat.arrived(0)
    gat.norm_arrived()

    low = lane_low((halflen, LANES))
    lowq = lane_low((length, LANES))
    low8 = lane_low((8, LANES))

    def tiles(ref):
        found = []
        for p in range(row_count // 2):
            left = ref[2 * p, length:, :].astype(f32)
            right = ref[2 * p + 1, length:, :].astype(f32)
            middle = swap(ref[2 * p + 1, :length, :].astype(f32))
            left = jnp.concatenate([left, swap(left)], 0)
            right = jnp.concatenate([swap(right), right], 0)
            found += [ref[2 * p, :length, :].astype(f32), jnp.where(lowq, left, middle),
                      jnp.where(lowq, middle, right)]
        return found

    def norm_tile(n):
        p, place = n // 3, n % 3
        if place == 0:
            return s.ng[2 * p, :, :LANES]
        middle = swap(s.ng[2 * p + 1, :, :LANES])
        if place == 1:
            return jnp.where(low8, s.ng[2 * p, :, LANES:], middle)
        return jnp.where(low8, middle, swap(s.ng[2 * p + 1, :, LANES:]))

    xt = tiles(s.xg)
    mean = sum(jnp.sum(t, 1, keepdims=True) for t in xt) / width
    spread = sum(jnp.sum(t * t, 1, keepdims=True) for t in xt) / width - mean * mean
    rstd = lax.rsqrt(spread + norm_eps)
    for n in range(len(xt)):
        cols = slice(n * LANES, (n + 1) * LANES)
        gain = norm_tile(n)
        value = (xt[n] - mean) * rstd
        s.normed[:, cols] = value
        first = (value * gain[0:1] + gain[1:2]).astype(bf16)
        second = (value * gain[2:3] + gain[3:4]).astype(bf16)
        s.fi[:, cols] = first
        s.si[:, cols] = second
        s.fit[cols, :] = first.T
        s.sit[cols, :] = second.T
    s.rstd[...] = jnp.broadcast_to(rstd, (length, LANES))

    for k in range(1, row_count):
        gat.relay(1, k)
    gat.send_own(3)
    gat.forward(1)
    gat.relay(2, 1)
    gat.landed(0)
    gat.arrived(1)
    ct = tiles(s.cg)
    for n in range(len(ct)):
        cols = slice(n * LANES, (n + 1) * LANES)
        value = ct[n].astype(bf16)
        s.co[:, cols] = value
        s.cot[cols, :] = value.T
    gat.relay(2, 2)
    gat.landed(1)
    s.dcat[...] = mm(s.co[...], wp[...]).astype(bf16)
    lowb = lane_low((QBLOCK, LANES))
    scale = 1.0 / math.sqrt(HEAD_DIM)

    def pair_step(p):
        base = p * 3 * LANES
        out_at = slice(p * LANES, (p + 1) * LANES)
        packed = mm(s.fi[...], wq[:, base:base + 3 * LANES])
        t0, t1, t2 = (packed[:, n * LANES:(n + 1) * LANES] for n in range(3))
        query = turn(jnp.where(lowq, t0, t1), 1.0).astype(bf16)
        keys = turn(swap(jnp.where(lowq, t2, t0)), 1.0).astype(bf16)
        values = jnp.where(lowq, t1, t2).astype(bf16)
        grads = s.dcat[:, out_at]
        s.dk[...] = jnp.zeros_like(s.dk)
        s.dv[...] = jnp.zeros_like(s.dv)
        zero = jnp.zeros((), bf16)
        dqs = []
        for n, (start, lo, hi) in enumerate(spans):
            allowed = s.mask[n, :, :hi - lo] > 0.5
            qb, gb = query[start:hi], grads[start:hi]
            kw, vw = keys[lo:hi], values[lo:hi]
            mixed, dq = [], []
            for head in range(2):
                sel = lowb if head == 0 else jnp.logical_not(lowb)
                qm = jnp.where(sel, qb, zero)
                gm = jnp.where(sel, gb, zero)
                scores = jnp.where(allowed, mm_cols(qm, kw) * scale, mask_fill)
                logsum = jnp.log(jnp.sum(jnp.exp(scores), 1, keepdims=True))
                probs = jnp.exp(scores - logsum)
                weights = probs.astype(bf16)
                got = mm(weights, vw).astype(bf16)
                delta = jnp.sum(gm.astype(f32) * got.astype(f32), 1, keepdims=True)
                prod = mm_cols(gm, vw)
                score_grad = (probs * (prod - delta) * scale).astype(bf16)
                mixed.append(got)
                dq.append(mm(score_grad, kw))
                s.dk[lo:hi, :] += mm_rows(score_grad, qm)
                s.dv[lo:hi, :] += mm_rows(weights, gm)
            s.att[start:hi, out_at] = jnp.where(lowb, mixed[0], mixed[1])
            dqs.append(jnp.where(lowb, dq[0], dq[1]))
        dquery = turn(jnp.concatenate(dqs, 0), -1.0)
        dkeys = swap(turn(s.dk[...], -1.0))
        dvals = s.dv[...]
        s.pg[:, base:base + LANES] = jnp.where(lowq, dquery, dkeys).astype(bf16)
        s.pg[:, base + LANES:base + 2 * LANES] = jnp.where(lowq, dvals, dquery).astype(bf16)
        s.pg[:, base + 2 * LANES:base + 3 * LANES] = jnp.where(lowq, dkeys, dvals).astype(bf16)

    todo = [(2, k) for k in range(3, row_count)] + [(3, k) for k in range(1, row_count)]
    for p in range(attn // LANES):
        pair_step(p)
        if todo:
            gat.relay(*todo.pop(0))
    step = 2 * LANES

    def weight_grads(ref, left, right, size):
        count = size // step

        def one(n, carry):
            cols = pl.ds(pl.multiple_of(n * step, step), step)
            ref[:, cols] = mm(left[...], right[:, cols]).astype(bf16)
            return carry

        lax.fori_loop(0, count, one, 0)
        if size % step:
            cols = slice(count * step, size)
            ref[:, cols] = mm(left[...], right[:, cols]).astype(bf16)

    weight_grads(gq, s.fit, s.pg, s.pg.shape[1])
    red.start(0)
    while todo:
        gat.relay(*todo.pop(0))
    weight_grads(gp, s.cot, s.att, attn)
    red.start(1)
    for t in red.order:
        red.stage_far(0, t)
    gat.settle()
    gat.landed(2)
    gat.landed(3)
    for t in red.order:
        red.stage_far(1, t)

    def hidden_step(n, carry):
        cols = pl.ds(pl.multiple_of(n * step, step), step)
        value = mm(s.si[...], wu[:, cols])
        erf = 0.5 * (1.0 + lax.erf(value * inv_sqrt_two))
        s.act[:, cols] = (value * erf).astype(bf16)
        slope = erf + value * inv_sqrt_two_pi * jnp.exp(-0.5 * value * value)
        s.hg[:, cols] = (mm(s.co[...], wd[:, cols]) * slope).astype(bf16)
        return carry

    lax.fori_loop(0, hidden // step, hidden_step, 0)
    weight_grads(gd, s.cot, s.act, hidden)
    red.start(2)
    weight_grads(gu, s.sit, s.hg, hidden)
    red.start(3)
    for g in (2, 3):
        for t in red.order:
            red.stage_far(g, t)

    def put_tiles(ref, chunks):
        for p in range(row_count // 2):
            t0, t1, t2 = chunks[3 * p:3 * p + 3]
            ref[2 * p, :length, :] = t0.astype(bf16)
            ref[2 * p + 1, :length, :] = swap(jnp.where(lowq, t2, t1)).astype(bf16)
            ref[2 * p, length:, :] = jnp.where(
                low, t1[:halflen], swap(t1[halflen:])).astype(bf16)
            ref[2 * p + 1, length:, :] = jnp.where(
                low, swap(t2[:halflen]), t2[halflen:]).astype(bf16)

    def split(value):
        return [value[:, n * LANES:(n + 1) * LANES] for n in range(value.shape[1] // LANES)]

    out_tiles = []
    for n in range(width // step):
        cols = slice(n * step, (n + 1) * step)
        out_tiles += split(mm_cols(s.att[...], wp[cols, :]) + mm_cols(s.act[...], wd[cols, :]))
    put_tiles(s.outp, out_tiles)
    red.start_out()
    for t in red.order:
        red.stage_row(0, t)
    back1, back2 = 0.0, 0.0
    sums = []
    for n in range(width // step):
        cols = slice(n * step, (n + 1) * step)
        first = mm_cols(s.pg[...], wq[cols, :])
        second = mm_cols(s.hg[...], wu[cols, :])
        value = s.normed[:, cols]
        gains = jnp.concatenate([norm_tile(2 * n), norm_tile(2 * n + 1)], 1)
        four = jnp.concatenate(
            [jnp.sum(first * value, 0, keepdims=True), jnp.sum(first, 0, keepdims=True),
             jnp.sum(second * value, 0, keepdims=True), jnp.sum(second, 0, keepdims=True),
             jnp.zeros((4, step), f32)], 0)
        sums += split(four)
        both = gains[0:1] * first + gains[2:3] * second
        s.comb[:, cols] = both
        back1 = back1 + jnp.sum(both, 1, keepdims=True)
        back2 = back2 + jnp.sum(both * value, 1, keepdims=True)
    for p in range(row_count // 2):
        t0, t1, t2 = sums[3 * p:3 * p + 3]
        s.nrmp[2 * p, :, :LANES] = t0
        s.nrmp[2 * p, :, LANES:] = t1
        s.nrmp[2 * p + 1, :, :LANES] = swap(jnp.where(low8, t2, t1))
        s.nrmp[2 * p + 1, :, LANES:] = swap(t2)
    red.start_norm()
    grad_tiles = []
    factor = s.rstd[...]
    for n in range(width // LANES):
        cols = slice(n * LANES, (n + 1) * LANES)
        grad_tiles.append(factor * (
            s.comb[:, cols] - back1 / width - s.normed[:, cols] * (back2 / width)))
    put_tiles(s.gradp, grad_tiles)
    red.start_grad()

    red.outputs_out()
    for t in red.order:
        red.stage_row(1, t)
    red.finish(0)
    red.outputs_grad()
    for t in red.order:
        red.stage_row(2, t)
    red.finish(1)
    red.norm_rows()
    red.spread(0)
    for n, t in enumerate(red.order):
        red.stage_row(3, t)
        if n == 1:
            red.norm_cols()
        if n == last:
            red.finish(2)
    red.grads_home()
    red.spread(1)
    red.finish(3)
    red.norm_last()
    red.spread(2)
    red.spread(3)
    gat.drain()
    red.drain()


LISTS = ("whole", "part", "crecv", "fsend", "frecv", "zsend", "zrecv", "extra")


def layer_all(row_count, data_count, width, tok, cot, nrm, segs, freq, own):
    n = row_count
    bf16, f32 = jnp.bfloat16, jnp.float32
    dma = pltpu.SemaphoreType.DMA
    vmem = pl.BlockSpec(memory_space=pltpu.VMEM)
    anywhere = pl.BlockSpec(memory_space=pl.ANY)
    shares, rows, _ = tok.shape
    length = segs.shape[1]
    groups = len(own)
    groups_out = data_count // QUARTERS
    sizes = [w.shape[1] for w in own]
    local = own[0].shape[0]
    depth = local // QUARTERS
    block = (rows, LANES)
    small = nrm.shape
    attn, hidden = sizes[1], sizes[3]
    spec = {}

    def buffers(dtype, **shapes):
        for name, shape in shapes.items():
            spec[name] = pltpu.VMEM(shape, dtype)

    def each(name, lead):
        for g, size in enumerate(sizes):
            spec[f"{name}{g}"] = pltpu.VMEM(lead + (size,), bf16)

    def sems(**shapes):
        for name, shape in shapes.items():
            spec[name] = dma(shape)

    each("whole", (width,))
    each("part", (width,))
    each("crecv", (2, n, depth))
    for name in ("fsend", "frecv", "zsend", "zrecv"):
        each(name, (n, depth))
    each("extra", (groups_out, depth))
    buffers(bf16, xg=(n,) + block, cg=(n,) + block, hop=(shares,) + block,
            fi=(length, width), si=(length, width), co=(length, width),
            fit=(width, length), sit=(width, length), cot=(width, length),
            dcat=(length, attn), att=(length, attn), act=(length, hidden), hg=(length, hidden),
            pg=(length, sizes[0]), outp=(n,) + block, gradp=(n,) + block,
            oy=(n,) + block, od=(n,) + block, gy=(n,) + block, gd=(n,) + block,
            gh=(shares,) + block)
    buffers(f32, ng=(n,) + small, nrmp=(n,) + small, nz=(n,) + small, nc=small, nrm1=small,
            nrm2=small, nd=(data_count,) + small, mask=(length // QBLOCK, QBLOCK, WINDOW + QBLOCK),
            cosine=(length, LANES), sine=(length, LANES), rstd=(length, LANES),
            dk=(length, LANES), dv=(length, LANES), normed=(length, width),
            comb=(length, width))
    sems(nrm_s=(n,), nrm_r=(n,), x_s=(shares,), x_r=(n,), xy_s=(n,), xy_r=(n,),
         h_s=(shares,), h_r=(shares,), c_s=(shares,), c_r=(n,), cy_s=(n,), cy_r=(n,),
         loc=(5,), own_l=(groups,), z_s=(2, groups, n), z_r=(groups, n),
         f_s=(groups, n), f_r=(groups, n), m_s=(2, groups, n), m_r=(2, groups, n),
         oy_s=(n,), oy_r=(n,), oz_s=(n,), oz_r=(shares,), gy_s=(n,), gy_r=(n,),
         gz_s=(n,), gz_r=(shares,), gh_s=(shares,), gh_r=(shares,), nz_s=(n,), nz_r=(n,),
         nc_s=(1,), nc_r=(1,), nd_s=(data_count,), nd_r=(data_count,),
         pc_s=(2, groups, n), pc_r=(2, groups, n), pf_s=(groups, n), pf_r=(groups, n),
         pz_s=(groups, n), pz_r=(groups, n), e_s=(groups, groups_out), e_r=(groups, groups_out),
         a_s=(groups,), a_r=(groups,), b_s=(2, groups), b_r=(2, groups))
    return pl.pallas_call(
        functools.partial(layer_kernel, n, width, groups_out, tuple(spec)),
        out_shape=[
            jax.ShapeDtypeStruct((shares,) + block, bf16),
            jax.ShapeDtypeStruct((shares,) + block, bf16),
            jax.ShapeDtypeStruct(small, f32),
        ] + [jax.ShapeDtypeStruct((local, size), bf16) for size in sizes],
        in_specs=[anywhere] * 3 + [vmem] * 2 + [anywhere] * groups,
        out_specs=[vmem] * (3 + groups),
        scratch_shapes=list(spec.values()),
        compiler_params=pltpu.CompilerParams(
            collective_id=0, has_side_effects=True, vmem_limit_bytes=63 << 20
        ),
        name="layer",
    )(tok, cot, nrm, segs, freq, *own)


def pack_tokens(rows, length):
    blocks = rows.reshape(-1, length, rows.shape[1])
    ends = blocks[:, :, LANES:]
    joined = jnp.concatenate([ends[:, :length // 2], ends[:, length // 2:]], 2)
    return jnp.concatenate([blocks[:, :, :LANES], joined], 1)


def unpack_tokens(blocks, length):
    joined = blocks[:, length:]
    small = joined.shape[2] // 2
    ends = jnp.concatenate([joined[:, :, :small], joined[:, :, small:]], 1)
    return jnp.concatenate([blocks[:, :length], ends], 2).reshape(-1, LANES + small)


def on_device(
    tokens_in,
    out_cot,
    segments,
    norm_params,
    qkv_weight,
    proj_weight,
    up_weight,
    down_weight,
    norm_first,
    norm_second,
    qkv_first,
    qkv_second,
    proj_first,
    proj_second,
    up_first,
    up_second,
    down_first,
    down_second,
):
    row_count = lax.axis_size("row")
    data_count = lax.axis_size("dp")
    col_count = lax.axis_size("col")
    local_count, local_width = tokens_in.shape
    width = local_width * row_count
    length = segments.shape[1]
    shares = local_count // length
    bf16 = jnp.bfloat16

    own = (
        qkv_weight.astype(bf16),
        proj_weight.T.astype(bf16),
        down_weight.T.astype(bf16),
        up_weight.astype(bf16),
    )
    nrm = jnp.pad(norm_params, ((0, 4), (0, 2 * LANES - local_width)))
    half = ROT_DIM // 2
    freq = rotary_base ** (-2.0 * jnp.arange(half, dtype=jnp.float32) / ROT_DIM)
    freq = jnp.concatenate([freq, freq, jnp.zeros(HEAD_DIM - ROT_DIM, jnp.float32)])
    freq = jnp.broadcast_to(jnp.tile(freq, 2)[None], (8, LANES))
    out_sum, grad_sum, norm_sum, qkv_sum, proj_sum, down_sum, up_sum = layer_all(
        row_count, data_count, width, pack_tokens(tokens_in, length),
        pack_tokens(out_cot, length), nrm, segments, freq, own)

    output = (tokens_in.astype(jnp.float32)
              + unpack_tokens(out_sum, length).astype(jnp.float32)).astype(bf16)
    input_grad = (out_cot.astype(jnp.float32)
                  + unpack_tokens(grad_sum, length).astype(jnp.float32)).astype(bf16)
    norm_grad = norm_sum[:4, :local_width]
    qkv_grad = qkv_sum.astype(jnp.float32)
    up_grad = up_sum.astype(jnp.float32)
    proj_grad = proj_sum.astype(jnp.float32).T
    down_grad = down_sum.astype(jnp.float32).T
    norm_new, norm_first_new, norm_second_new = adam_update(
        norm_params, norm_first, norm_second, norm_grad, 0.0
    )
    qkv_new, qkv_first_new, qkv_second_new = adam_update(
        qkv_weight, qkv_first, qkv_second, qkv_grad, decay_rate
    )
    proj_new, proj_first_new, proj_second_new = adam_update(
        proj_weight, proj_first, proj_second, proj_grad, decay_rate
    )
    up_new, up_first_new, up_second_new = adam_update(
        up_weight, up_first, up_second, up_grad, decay_rate
    )
    down_new, down_first_new, down_second_new = adam_update(
        down_weight, down_first, down_second, down_grad, decay_rate
    )
    return (
        output,
        input_grad,
        norm_grad,
        qkv_grad,
        proj_grad,
        up_grad,
        down_grad,
        norm_new,
        qkv_new,
        proj_new,
        up_new,
        down_new,
        norm_first_new,
        norm_second_new,
        qkv_first_new,
        qkv_second_new,
        proj_first_new,
        proj_second_new,
        up_first_new,
        up_second_new,
        down_first_new,
        down_second_new,
    )


def solution(mesh):
    placed = (
        P(("dp", "col"), "row"),
        P(("dp", "col"), "row"),
        P("dp", None),
        P(None, "row"),
        P("row", "col"),
        P("col", "row"),
        P("row", "col"),
        P("col", "row"),
        P(None, "row"),
        P(None, "row"),
        P("row", "col"),
        P("row", "col"),
        P("col", "row"),
        P("col", "row"),
        P("row", "col"),
        P("row", "col"),
        P("col", "row"),
        P("col", "row"),
    )
    return jax.shard_map(
        on_device,
        mesh=mesh,
        in_specs=placed,
        out_specs=(
            P(("dp", "col"), "row"),
            P(("dp", "col"), "row"),
            P(None, "row"),
            P("row", "col"),
            P("col", "row"),
            P("row", "col"),
            P("col", "row"),
            P(None, "row"),
            P("row", "col"),
            P("col", "row"),
            P("row", "col"),
            P("col", "row"),
            P(None, "row"),
            P(None, "row"),
            P("row", "col"),
            P("row", "col"),
            P("col", "row"),
            P("col", "row"),
            P("row", "col"),
            P("row", "col"),
            P("col", "row"),
            P("col", "row"),
        ),
        check_vma=False,
    )
```

```python
import functools
import math
import types

import jax
import jax.numpy as jnp
from jax import lax
from jax.experimental import pallas as pl
from jax.experimental.pallas import tpu as pltpu
from jax.sharding import PartitionSpec as P

D = 768
HEAD_DIM = 64
ROT_DIM = 16
SEQ_LEN = 512
STEP = 3


norm_eps = 1e-05
rotary_base = 10000.0
learn_rate = 0.01
beta_first = 0.9
beta_second = 0.95
adam_eps = 1e-08
decay_rate = 0.1
mask_fill = -1e30
inv_sqrt_two = 0.7071067811865476
inv_sqrt_two_pi = 0.3989422804014327


def adam_update(weight, first, second, grad, decay):
    first_new = beta_first * first + (1.0 - beta_first) * grad
    second_new = beta_second * second + (1.0 - beta_second) * grad * grad
    first_hat = first_new / (1.0 - beta_first**STEP)
    second_hat = second_new / (1.0 - beta_second**STEP)
    weight_new = weight - learn_rate * (
        first_hat / (jnp.sqrt(second_hat) + adam_eps) + decay * weight
    )
    return (weight_new, first_new, second_new)


MESH = pl.DeviceIdType.MESH
LANES = 128
QUARTERS = 4
WINDOW = 256
QBLOCK = 128


def remote(src, dst, send_sem, recv_sem, device):
    return pltpu.make_async_remote_copy(
        src_ref=src,
        dst_ref=dst,
        send_sem=send_sem,
        recv_sem=recv_sem,
        device_id=device,
        device_id_type=MESH,
    )


def places(row_count):
    data, row, col = lax.axis_index("dp"), lax.axis_index("row"), lax.axis_index("col")
    quarter = lax.rem(data, QUARTERS)
    far = data - quarter + lax.rem(quarter + 2, QUARTERS)
    mate = data + 1 - 2 * lax.rem(quarter, 2)
    return data, row, col, quarter, far, mate


def greet(peers):
    barrier = pltpu.get_barrier_semaphore()
    for peer in peers:
        pl.semaphore_signal(barrier, inc=1, device_id=peer, device_id_type=MESH)
    pl.semaphore_wait(barrier, len(peers))


def gatherer(row_count, at, tok, cot, nrm, own_w, all_w, s):
    data, row, col, quarter, far, mate = at
    shares = tok.shape[0]
    other = 1 - col
    home = lax.div(row, shares)
    groups = len(own_w)
    local = own_w[0].shape[0]
    depth = local // QUARTERS
    others = [lax.rem(row + k, row_count) for k in range(1, row_count)]

    def rows(src, part):
        return pl.ds(pl.multiple_of(src * local + part * depth, depth), depth)

    def step_copy(g, src, up):
        ref = all_w[g].at[rows(src, quarter)]
        return remote(ref, ref, s.z_s.at[int(up), g, src], s.z_r.at[g, src],
                      (data, row + 1 if up else row - 1, col))

    def own_copy(g, up):
        return remote(own_w[g].at[rows(0, quarter)], all_w[g].at[rows(row, quarter)],
                      s.z_s.at[int(up), g, row], s.z_r.at[g, row],
                      (data, row + 1 if up else row - 1, col))

    def own_local(g):
        dest = all_w[g].at[pl.ds(pl.multiple_of(row * local, local), local)]
        return pltpu.make_async_copy(own_w[g], dest, s.own_l.at[g])

    def far_copy(g, src):
        ref = all_w[g].at[rows(src, quarter)]
        return remote(ref, ref, s.f_s.at[g, src], s.f_r.at[g, src], (far, row, col))

    def far_wait(g, src):
        ref = all_w[g].at[rows(src, lax.rem(quarter + 2, QUARTERS))]
        remote(ref, ref, s.f_s.at[g, src], s.f_r.at[g, src], (far, row, col)).wait_recv()

    def mate_copy(g, src, second):
        part = lax.rem(quarter + 2, QUARTERS) if second else quarter
        ref = all_w[g].at[rows(src, part)]
        return remote(ref, ref, s.m_s.at[int(second), g, src], s.m_r.at[int(second), g, src],
                      (mate, row, col))

    def mate_wait(g, src, second):
        theirs = quarter + 1 - 2 * lax.rem(quarter, 2)
        part = lax.rem(theirs + 2, QUARTERS) if second else theirs
        ref = all_w[g].at[rows(src, part)]
        remote(ref, ref, s.m_s.at[int(second), g, src], s.m_r.at[int(second), g, src],
               (mate, row, col)).wait_recv()

    def norm_copy(k):
        return remote(nrm, s.ng.at[row], s.nrm_s.at[k], s.nrm_r.at[row], (data, others[k], col))

    def norm_wait(k):
        remote(nrm, s.ng.at[others[k]], s.nrm_s.at[k], s.nrm_r.at[others[k]],
               (data, others[k], col)).wait_recv()

    def norm_local():
        return pltpu.make_async_copy(nrm, s.ng.at[row], s.loc.at[2])

    def token_copy(j):
        return remote(tok.at[j], s.xg.at[row], s.x_s.at[j], s.x_r.at[row],
                      (data, col * shares + j, col))

    def token_local(j):
        return pltpu.make_async_copy(tok.at[j], s.xg.at[row], s.loc.at[0])

    def hop_copy(j):
        return remote(cot.at[j], s.hop.at[j], s.h_s.at[j], s.h_r.at[j], (data, row, other))

    def cot_copy(j):
        return remote(s.hop.at[j], s.cg.at[row], s.c_s.at[j], s.c_r.at[row],
                      (data, other * shares + j, col))

    def cot_local(j):
        return pltpu.make_async_copy(s.hop.at[j], s.cg.at[row], s.loc.at[1])

    def x_wait(src):
        remote(tok.at[0], s.xg.at[src], s.x_s.at[0], s.x_r.at[src],
               (data, src, col)).wait_recv()

    def c_wait(src):
        remote(tok.at[0], s.cg.at[src], s.c_s.at[0], s.c_r.at[src],
               (data, src, col)).wait_recv()

    def across(which, src):
        ref, send, recv = ((s.xg, s.xy_s, s.xy_r), (s.cg, s.cy_s, s.cy_r))[which]
        return remote(ref.at[src], ref.at[src], send.at[src], recv.at[src],
                      (data, row, other))

    mains = (col == home, col != home)

    def begin():
        for k in range(row_count - 1):
            norm_copy(k).start()
        norm_local().start()
        for j in range(shares):
            @pl.when(col * shares + j != row)
            def _():
                token_copy(j).start()

            @pl.when(col * shares + j == row)
            def _():
                token_local(j).start()
            hop_copy(j).start()
        for g in range(groups):
            own_local(g).start()

    def send_own(g):
        @pl.when(row + 1 < row_count)
        def _():
            own_copy(g, True).start()

        @pl.when(row > 0)
        def _():
            own_copy(g, False).start()

    def cot_hop():
        for j in range(shares):
            hop_copy(j).wait_recv()

            @pl.when(other * shares + j != row)
            def _():
                cot_copy(j).start()

            @pl.when(other * shares + j == row)
            def _():
                cot_local(j).start()

    def forward(which):
        @pl.when(mains[which])
        def _():
            (token_local, cot_local)[which](0).wait()
            across(which, row).start()
            for src in others:
                (x_wait, c_wait)[which](src)
                across(which, src).start()

    def arrived(which):
        @pl.when(jnp.logical_not(mains[which]))
        def _():
            for src in range(row_count):
                across(which, src).wait_recv()

    def norm_arrived():
        norm_local().wait()
        for k in range(row_count - 1):
            norm_wait(k)

    pending = []

    def settle():
        for g, k, below in pending:
            src = row - k if below else row + k

            @pl.when(src >= 0 if below else src < row_count)
            def _():
                far_wait(g, src)
                mate_copy(g, src, True).start()
        pending.clear()

    def relay(g, k):
        now = []
        for below in (True, False):
            src = row - k if below else row + k

            @pl.when(src >= 0 if below else src < row_count)
            def _():
                step_copy(g, src, below).wait_recv()
                onward = row + 1 < row_count if below else row > 0

                @pl.when(onward)
                def _():
                    step_copy(g, src, below).start()
                far_copy(g, src).start()
                mate_copy(g, src, False).start()
            now.append((g, k, below))
        settle()
        pending.extend(now)

    def landed(g):
        own_local(g).wait()
        for k in range(1, row_count):
            for second in (False, True):
                mate_wait(g, others[k - 1], second)

    def drain():
        for which in range(2):
            @pl.when(mains[which])
            def _():
                for src in range(row_count):
                    across(which, src).wait_send()
        for k in range(row_count - 1):
            norm_copy(k).wait_send()
        for j in range(shares):
            @pl.when(col * shares + j != row)
            def _():
                token_copy(j).wait_send()

            @pl.when(other * shares + j != row)
            def _():
                cot_copy(j).wait_send()
            hop_copy(j).wait_send()
        for g in range(groups):
            @pl.when(row + 1 < row_count)
            def _():
                own_copy(g, True).wait_send()

            @pl.when(row > 0)
            def _():
                own_copy(g, False).wait_send()
            for k in range(1, row_count):
                for below in (True, False):
                    src = row - k if below else row + k

                    @pl.when(src >= 0 if below else src < row_count)
                    def _():
                        onward = row + 1 < row_count if below else row > 0

                        @pl.when(onward)
                        def _():
                            step_copy(g, src, below).wait_send()
                        far_copy(g, src).wait_send()
                        for second in (False, True):
                            mate_copy(g, src, second).wait_send()

    return types.SimpleNamespace(
        begin=begin, send_own=send_own, cot_hop=cot_hop, forward=forward, arrived=arrived,
        norm_arrived=norm_arrived, settle=settle, relay=relay, landed=landed, drain=drain)


def reducer(row_count, groups_out, at, parts, total, out_t, grad_t, nrm_t, s):
    data, row, col, quarter, far, mate = at
    groups = len(parts)
    shares = out_t.shape[0]
    other = 1 - col
    home = lax.div(row, shares)
    local = parts[0].shape[0] // row_count
    depth = local // QUARTERS
    data_count = QUARTERS * groups_out
    block = lax.div(data, QUARTERS)
    others = [lax.rem(row + k, row_count) for k in range(1, row_count)]
    order = others + [row]
    wider = [lax.rem(data + QUARTERS * k, data_count) for k in range(1, groups_out)]
    everyone = [lax.rem(data + k, data_count) for k in range(1, data_count)]
    f32, bf16 = jnp.float32, jnp.bfloat16
    half = lax.rem(quarter + 2, QUARTERS)
    theirs = quarter + 1 - 2 * lax.rem(quarter, 2)
    theirs_half = lax.rem(theirs + 2, QUARTERS)
    slot = row - home * shares

    def rows(t, part):
        return pl.ds(pl.multiple_of(t * local + part * depth, depth), depth)

    def norm_z(k):
        return remote(s.nrmp.at[others[k]], s.nz.at[row], s.nz_s.at[k], s.nz_r.at[row],
                      (data, others[k], col))

    def norm_z_wait(k):
        remote(s.nrmp.at[0], s.nz.at[others[k]], s.nz_s.at[k], s.nz_r.at[others[k]],
               (data, others[k], col)).wait_recv()

    def norm_c():
        return remote(s.nrm1, s.nc, s.nc_s.at[0], s.nc_r.at[0], (data, row, other))

    def norm_d(k):
        return remote(s.nrm2, s.nd.at[data], s.nd_s.at[k], s.nd_r.at[data],
                      (everyone[k], row, col))

    def norm_d_wait(k):
        remote(s.nrm2, s.nd.at[everyone[k]], s.nd_s.at[k], s.nd_r.at[everyone[k]],
               (everyone[k], row, col)).wait_recv()

    def out_y(t):
        return remote(s.outp.at[t], s.oy.at[t], s.oy_s.at[t], s.oy_r.at[t], (data, row, other))

    def grad_y(t):
        return remote(s.gradp.at[t], s.gy.at[t], s.gy_s.at[t], s.gy_r.at[t],
                      (data, row, other))

    def out_z(t):
        return remote(s.od.at[t], out_t.at[slot], s.oz_s.at[t], s.oz_r.at[slot],
                      (data, t, col))

    def out_local():
        return pltpu.make_async_copy(s.od.at[row], out_t.at[slot], s.loc.at[3])

    def out_z_wait(j):
        remote(s.od.at[0], out_t.at[j], s.oz_s.at[0], s.oz_r.at[j],
               (data, row, col)).wait_recv()

    def grad_z(t):
        return remote(s.gd.at[t], s.gh.at[slot], s.gz_s.at[t], s.gz_r.at[slot],
                      (data, t, col))

    def grad_local():
        return pltpu.make_async_copy(s.gd.at[row], s.gh.at[slot], s.loc.at[4])

    def grad_z_wait(j):
        remote(s.gd.at[0], s.gh.at[j], s.gz_s.at[0], s.gz_r.at[j],
               (data, row, col)).wait_recv()

    def grad_h(j):
        return remote(s.gh.at[j], grad_t.at[j], s.gh_s.at[j], s.gh_r.at[j], (data, row, other))

    def mate_part(g, t, second):
        part = theirs_half if second else theirs
        return remote(parts[g].at[rows(t, part)], s.crecv[g].at[int(second), t],
                      s.pc_s.at[int(second), g, t], s.pc_r.at[int(second), g, t],
                      (mate, row, col))

    def far_part(g, t):
        return remote(s.fsend[g].at[t], s.frecv[g].at[t], s.pf_s.at[g, t], s.pf_r.at[g, t],
                      (far, row, col))

    def row_part(g, t):
        return remote(s.zsend[g].at[t], s.zrecv[g].at[row], s.pz_s.at[g, t], s.pz_r.at[g, row],
                      (data, t, col))

    def row_wait(g, src):
        remote(s.zsend[g].at[src], s.zrecv[g].at[src], s.pz_s.at[g, src], s.pz_r.at[g, src],
               (data, src, col)).wait_recv()

    def wide_part(g, k):
        return remote(total[g].at[rows(0, quarter)], s.extra[g].at[block],
                      s.e_s.at[g, k], s.e_r.at[g, block], (wider[k], row, col))

    def wide_wait(g, k):
        src = lax.div(wider[k], QUARTERS)
        remote(total[g].at[rows(0, quarter)], s.extra[g].at[src],
               s.e_s.at[g, k], s.e_r.at[g, src], (wider[k], row, col)).wait_recv()

    def far_sum(g):
        ref = total[g].at[rows(0, quarter)]
        return remote(ref, ref, s.a_s.at[g], s.a_r.at[g], (far, row, col))

    def far_sum_wait(g):
        ref = total[g].at[rows(0, half)]
        remote(ref, ref, s.a_s.at[g], s.a_r.at[g], (far, row, col)).wait_recv()

    def mate_sum(g, second):
        ref = total[g].at[rows(0, half if second else quarter)]
        return remote(ref, ref, s.b_s.at[int(second), g], s.b_r.at[int(second), g],
                      (mate, row, col))

    def mate_sum_wait(g, second):
        ref = total[g].at[rows(0, theirs_half if second else theirs)]
        remote(ref, ref, s.b_s.at[int(second), g], s.b_r.at[int(second), g],
               (mate, row, col)).wait_recv()

    o_main = col == home
    g_main = col != home

    def start(g):
        for t in order:
            mate_part(g, t, True).start()
        for t in order:
            mate_part(g, t, False).start()

    def start_out():
        @pl.when(jnp.logical_not(o_main))
        def _():
            for t in order:
                out_y(t).start()

    def start_grad():
        @pl.when(jnp.logical_not(g_main))
        def _():
            for t in order:
                grad_y(t).start()

    def start_norm():
        for k in range(row_count - 1):
            norm_z(k).start()

    def stage_far(g, t):
        mate_part(g, t, True).wait_recv()
        own = parts[g][rows(t, half), :].astype(f32)
        s.fsend[g][t] = (own + s.crecv[g][1, t].astype(f32)).astype(bf16)
        far_part(g, t).start()

    def stage_row(g, t):
        mate_part(g, t, False).wait_recv()
        far_part(g, t).wait_recv()
        mine = parts[g][rows(t, quarter), :].astype(f32)
        mine = mine + s.crecv[g][0, t].astype(f32) + s.frecv[g][t].astype(f32)
        s.zsend[g][t] = mine.astype(bf16)
        if t is not row:
            row_part(g, t).start()

    def outputs_out():
        @pl.when(o_main)
        def _():
            for t in order:
                out_y(t).wait_recv()
                s.od[t] = (s.outp[t].astype(f32) + s.oy[t].astype(f32)).astype(bf16)
                if t is row:
                    out_local().start()
                else:
                    out_z(t).start()

    def outputs_grad():
        @pl.when(g_main)
        def _():
            for t in order:
                grad_y(t).wait_recv()
                s.gd[t] = (s.gradp[t].astype(f32) + s.gy[t].astype(f32)).astype(bf16)
                if t is row:
                    grad_local().start()
                else:
                    grad_z(t).start()

    def grads_home():
        for j in range(shares):
            @pl.when(other * shares + j != row)
            def _():
                grad_z_wait(j)

            @pl.when(other * shares + j == row)
            def _():
                grad_local().wait()
            grad_h(j).start()

    def norm_rows():
        acc = s.nrmp[row]
        for k in range(row_count - 1):
            norm_z_wait(k)
            acc = acc + s.nz[others[k]]
        s.nrm1[...] = acc
        norm_c().start()

    def norm_cols():
        norm_c().wait_recv()
        s.nrm2[...] = s.nrm1[...] + s.nc[...]
        for k in range(len(everyone)):
            norm_d(k).start()

    def norm_last():
        acc = s.nrm2[...]
        for k in range(len(everyone)):
            norm_d_wait(k)
            acc = acc + s.nd[everyone[k]]
        nrm_t[...] = acc

    def finish(g):
        acc = s.zsend[g][row].astype(f32)
        for src in others:
            row_wait(g, src)
            acc = acc + s.zrecv[g][src].astype(f32)
        total[g][rows(0, quarter), :] = acc.astype(bf16)
        if wider:
            for k in range(len(wider)):
                wide_part(g, k).start()
            for k in range(len(wider)):
                wide_wait(g, k)
                acc = acc + s.extra[g][lax.div(wider[k], QUARTERS)].astype(f32)
            for k in range(len(wider)):
                wide_part(g, k).wait_send()
            total[g][rows(0, quarter), :] = acc.astype(bf16)
        far_sum(g).start()
        mate_sum(g, False).start()

    def spread(g):
        far_sum_wait(g)
        mate_sum(g, True).start()

    def drain():
        @pl.when(jnp.logical_not(o_main))
        def _():
            for t in range(row_count):
                out_y(t).wait_send()

        @pl.when(jnp.logical_not(g_main))
        def _():
            for t in range(row_count):
                grad_y(t).wait_send()

        @pl.when(o_main)
        def _():
            out_local().wait()
            for t in others:
                out_z(t).wait_send()

        @pl.when(g_main)
        def _():
            for t in others:
                grad_z(t).wait_send()
        for j in range(shares):
            @pl.when(col * shares + j != row)
            def _():
                out_z_wait(j)
            grad_h(j).wait()
        for k in range(row_count - 1):
            norm_z(k).wait_send()
        norm_c().wait_send()
        for k in range(len(everyone)):
            norm_d(k).wait_send()
        for g in range(groups):
            for t in range(row_count):
                for second in (False, True):
                    mate_part(g, t, second).wait_send()
                far_part(g, t).wait_send()
            for t in others:
                row_part(g, t).wait_send()
            far_sum(g).wait_send()
            for second in (False, True):
                mate_sum(g, second).wait_send()
                mate_sum_wait(g, second)

    return types.SimpleNamespace(
        order=order, everyone=everyone, start=start, start_out=start_out, start_grad=start_grad,
        start_norm=start_norm, stage_far=stage_far, stage_row=stage_row,
        outputs_out=outputs_out, outputs_grad=outputs_grad, grads_home=grads_home,
        norm_rows=norm_rows, norm_cols=norm_cols, norm_last=norm_last, finish=finish,
        spread=spread, drain=drain)


def lane_low(shape):
    return lax.broadcasted_iota(jnp.int32, shape, len(shape) - 1) < HEAD_DIM


def swap(tile):
    return pltpu.roll(tile, HEAD_DIM, 1)


def layer_kernel(row_count, width, groups_out, names, tok, cotan, nrm, seg_ref, freq_ref,
                 w0, w1, w2, w3, out_t, grad_t, nrm_t, r0, r1, r2, r3, *scratch):
    s = types.SimpleNamespace()
    for name, ref in zip(names, scratch):
        if name[-1].isdigit() and name[:-1] in LISTS:
            vars(s).setdefault(name[:-1], []).append(ref)
        else:
            setattr(s, name, ref)
    f32, bf16 = jnp.float32, jnp.bfloat16
    at = places(row_count)
    data, row, col, quarter, far, mate = at
    gat = gatherer(row_count, at, tok, cotan, nrm, (w0, w1, w2, w3), s.whole, s)
    red = reducer(row_count, groups_out, at, s.part, (r0, r1, r2, r3), out_t, grad_t, nrm_t, s)
    wq, wp, wd, wu = s.whole
    gq, gp, gd, gu = s.part
    length = s.xg.shape[1] * 2 // 3
    halflen = length // 2
    attn = wp.shape[1]
    hidden = wu.shape[1]
    last = row_count - 1

    greet([(data, lax.rem(row + k, row_count), col) for k in range(1, row_count)]
          + [(data, row, 1 - col)] + [(t, row, col) for t in red.everyone])

    def mm(a, b):
        return jnp.dot(a, b, preferred_element_type=f32)

    def mm_cols(a, b):
        return lax.dot_general(a, b, (((1,), (1,)), ((), ())), preferred_element_type=f32)

    def mm_rows(a, b):
        return lax.dot_general(a, b, (((0,), (0,)), ((), ())), preferred_element_type=f32)

    gat.begin()
    gat.send_own(0)
    gat.send_own(1)

    seg_row = seg_ref[pl.ds(row, 1), :].astype(f32)
    seg_col = jnp.broadcast_to(seg_row, (8, length)).T[:, 0:1]
    spans, pos = [], []
    for i in range(length // QBLOCK):
        spans.append((i * QBLOCK, max(0, i * QBLOCK - WINDOW), (i + 1) * QBLOCK))
    for n, (start, lo, hi) in enumerate(spans):
        shape = (QBLOCK, hi - lo)
        qi = lax.broadcasted_iota(jnp.int32, shape, 0) + start
        ki = lax.broadcasted_iota(jnp.int32, shape, 1) + lo
        allowed = (seg_col[start:hi] == seg_row[:, lo:hi]) & (ki <= qi)
        seen = jnp.where(allowed, 1.0, 0.0)
        s.mask[n, :, :hi - lo] = seen
        pos.append(jnp.sum(seen, 1, keepdims=True) - 1.0)
    angle = jnp.concatenate(pos, 0) * freq_ref[0:1, :]
    s.cosine[...] = jnp.cos(angle)
    s.sine[...] = jnp.sin(angle)
    lane = lax.rem(lax.broadcasted_iota(jnp.int32, (length, LANES), 1), HEAD_DIM)
    half = ROT_DIM // 2

    def turn(tile, sign):
        sine = s.sine[...]
        up = jnp.where(lane < half, -sine, 0.0)
        down = jnp.where((lane >= half) & (lane < ROT_DIM), sine, 0.0)
        return (tile * s.cosine[...] + sign * (pltpu.roll(tile, LANES - half, 1) * up
                                               + pltpu.roll(tile, half, 1) * down))

    gat.cot_hop()
    gat.relay(0, 1)
    gat.forward(0)
    gat.send_own(2)
    for k in range(2, row_count):
        gat.relay(0, k)
    gat.arrived(0)
    gat.norm_arrived()

    low = lane_low((halflen, LANES))
    lowq = lane_low((length, LANES))
    low8 = lane_low((8, LANES))

    def tiles(ref):
        found = []
        for p in range(row_count // 2):
            left = ref[2 * p, length:, :].astype(f32)
            right = ref[2 * p + 1, length:, :].astype(f32)
            middle = swap(ref[2 * p + 1, :length, :].astype(f32))
            left = jnp.concatenate([left, swap(left)], 0)
            right = jnp.concatenate([swap(right), right], 0)
            found += [ref[2 * p, :length, :].astype(f32), jnp.where(lowq, left, middle),
                      jnp.where(lowq, middle, right)]
        return found

    def norm_tile(n):
        p, place = n // 3, n % 3
        if place == 0:
            return s.ng[2 * p, :, :LANES]
        middle = swap(s.ng[2 * p + 1, :, :LANES])
        if place == 1:
            return jnp.where(low8, s.ng[2 * p, :, LANES:], middle)
        return jnp.where(low8, middle, swap(s.ng[2 * p + 1, :, LANES:]))

    xt = tiles(s.xg)
    mean = sum(jnp.sum(t, 1, keepdims=True) for t in xt) / width
    spread = sum(jnp.sum(t * t, 1, keepdims=True) for t in xt) / width - mean * mean
    rstd = lax.rsqrt(spread + norm_eps)
    for n in range(len(xt)):
        cols = slice(n * LANES, (n + 1) * LANES)
        gain = norm_tile(n)
        value = (xt[n] - mean) * rstd
        s.normed[:, cols] = value
        first = (value * gain[0:1] + gain[1:2]).astype(bf16)
        second = (value * gain[2:3] + gain[3:4]).astype(bf16)
        s.fi[:, cols] = first
        s.si[:, cols] = second
        s.fit[cols, :] = first.T
        s.sit[cols, :] = second.T
    s.rstd[...] = jnp.broadcast_to(rstd, (length, LANES))

    for k in range(1, row_count):
        gat.relay(1, k)
    gat.send_own(3)
    gat.forward(1)
    gat.relay(2, 1)
    gat.landed(0)
    gat.arrived(1)
    ct = tiles(s.cg)
    for n in range(len(ct)):
        cols = slice(n * LANES, (n + 1) * LANES)
        value = ct[n].astype(bf16)
        s.co[:, cols] = value
        s.cot[cols, :] = value.T
    gat.relay(2, 2)
    gat.landed(1)
    s.dcat[...] = mm(s.co[...], wp[...]).astype(bf16)
    lowb = lane_low((QBLOCK, LANES))
    scale = 1.0 / math.sqrt(HEAD_DIM)

    def pair_step(p):
        base = p * 3 * LANES
        out_at = slice(p * LANES, (p + 1) * LANES)
        packed = mm(s.fi[...], wq[:, base:base + 3 * LANES])
        t0, t1, t2 = (packed[:, n * LANES:(n + 1) * LANES] for n in range(3))
        query = turn(jnp.where(lowq, t0, t1), 1.0).astype(bf16)
        keys = turn(swap(jnp.where(lowq, t2, t0)), 1.0).astype(bf16)
        values = jnp.where(lowq, t1, t2).astype(bf16)
        grads = s.dcat[:, out_at]
        s.dk[...] = jnp.zeros_like(s.dk)
        s.dv[...] = jnp.zeros_like(s.dv)
        zero = jnp.zeros((), bf16)
        dqs = []
        for n, (start, lo, hi) in enumerate(spans):
            allowed = s.mask[n, :, :hi - lo] > 0.5
            qb, gb = query[start:hi], grads[start:hi]
            kw, vw = keys[lo:hi], values[lo:hi]
            mixed, dq = [], []
            for head in range(2):
                sel = lowb if head == 0 else jnp.logical_not(lowb)
                qm = jnp.where(sel, qb, zero)
                gm = jnp.where(sel, gb, zero)
                scores = jnp.where(allowed, mm_cols(qm, kw) * scale, mask_fill)
                logsum = jnp.log(jnp.sum(jnp.exp(scores), 1, keepdims=True))
                probs = jnp.exp(scores - logsum)
                weights = probs.astype(bf16)
                got = mm(weights, vw).astype(bf16)
                delta = jnp.sum(gm.astype(f32) * got.astype(f32), 1, keepdims=True)
                prod = mm_cols(gm, vw)
                score_grad = (probs * (prod - delta) * scale).astype(bf16)
                mixed.append(got)
                dq.append(mm(score_grad, kw))
                s.dk[lo:hi, :] += mm_rows(score_grad, qm)
                s.dv[lo:hi, :] += mm_rows(weights, gm)
            s.att[start:hi, out_at] = jnp.where(lowb, mixed[0], mixed[1])
            dqs.append(jnp.where(lowb, dq[0], dq[1]))
        dquery = turn(jnp.concatenate(dqs, 0), -1.0)
        dkeys = swap(turn(s.dk[...], -1.0))
        dvals = s.dv[...]
        s.pg[:, base:base + LANES] = jnp.where(lowq, dquery, dkeys).astype(bf16)
        s.pg[:, base + LANES:base + 2 * LANES] = jnp.where(lowq, dvals, dquery).astype(bf16)
        s.pg[:, base + 2 * LANES:base + 3 * LANES] = jnp.where(lowq, dkeys, dvals).astype(bf16)

    todo = [(2, k) for k in range(3, row_count)] + [(3, k) for k in range(1, row_count)]
    for p in range(attn // LANES):
        pair_step(p)
        if todo:
            gat.relay(*todo.pop(0))
    step = 2 * LANES

    def weight_grads(ref, left, right, size):
        count = size // step

        def one(n, carry):
            cols = pl.ds(pl.multiple_of(n * step, step), step)
            ref[:, cols] = mm(left[...], right[:, cols]).astype(bf16)
            return carry

        lax.fori_loop(0, count, one, 0)
        if size % step:
            cols = slice(count * step, size)
            ref[:, cols] = mm(left[...], right[:, cols]).astype(bf16)

    weight_grads(gq, s.fit, s.pg, s.pg.shape[1])
    red.start(0)
    while todo:
        gat.relay(*todo.pop(0))
    weight_grads(gp, s.cot, s.att, attn)
    red.start(1)
    for t in red.order:
        red.stage_far(0, t)
    for t in red.order:
        red.stage_far(1, t)
    gat.settle()
    gat.landed(2)
    gat.landed(3)

    def hidden_step(n, carry):
        cols = pl.ds(pl.multiple_of(n * step, step), step)
        value = mm(s.si[...], wu[:, cols])
        erf = 0.5 * (1.0 + lax.erf(value * inv_sqrt_two))
        s.act[:, cols] = (value * erf).astype(bf16)
        slope = erf + value * inv_sqrt_two_pi * jnp.exp(-0.5 * value * value)
        s.hg[:, cols] = (mm(s.co[...], wd[:, cols]) * slope).astype(bf16)
        return carry

    lax.fori_loop(0, hidden // step, hidden_step, 0)
    weight_grads(gd, s.cot, s.act, hidden)
    red.start(2)
    for t in red.order:
        red.stage_row(0, t)
    for t in red.order:
        red.stage_far(2, t)
    weight_grads(gu, s.sit, s.hg, hidden)
    red.start(3)
    for t in red.order:
        red.stage_row(1, t)
    for t in red.order:
        red.stage_far(3, t)

    def put_tiles(ref, chunks):
        for p in range(row_count // 2):
            t0, t1, t2 = chunks[3 * p:3 * p + 3]
            ref[2 * p, :length, :] = t0.astype(bf16)
            ref[2 * p + 1, :length, :] = swap(jnp.where(lowq, t2, t1)).astype(bf16)
            ref[2 * p, length:, :] = jnp.where(
                low, t1[:halflen], swap(t1[halflen:])).astype(bf16)
            ref[2 * p + 1, length:, :] = jnp.where(
                low, swap(t2[:halflen]), t2[halflen:]).astype(bf16)

    def split(value):
        return [value[:, n * LANES:(n + 1) * LANES] for n in range(value.shape[1] // LANES)]

    out_tiles = []
    for n in range(width // step):
        cols = slice(n * step, (n + 1) * step)
        out_tiles += split(mm_cols(s.att[...], wp[cols, :]) + mm_cols(s.act[...], wd[cols, :]))
    put_tiles(s.outp, out_tiles)
    red.start_out()
    back1, back2 = 0.0, 0.0
    sums = []
    for n in range(width // step):
        cols = slice(n * step, (n + 1) * step)
        first = mm_cols(s.pg[...], wq[cols, :])
        second = mm_cols(s.hg[...], wu[cols, :])
        value = s.normed[:, cols]
        gains = jnp.concatenate([norm_tile(2 * n), norm_tile(2 * n + 1)], 1)
        four = jnp.concatenate(
            [jnp.sum(first * value, 0, keepdims=True), jnp.sum(first, 0, keepdims=True),
             jnp.sum(second * value, 0, keepdims=True), jnp.sum(second, 0, keepdims=True),
             jnp.zeros((4, step), f32)], 0)
        sums += split(four)
        both = gains[0:1] * first + gains[2:3] * second
        s.comb[:, cols] = both
        back1 = back1 + jnp.sum(both, 1, keepdims=True)
        back2 = back2 + jnp.sum(both * value, 1, keepdims=True)
    for p in range(row_count // 2):
        t0, t1, t2 = sums[3 * p:3 * p + 3]
        s.nrmp[2 * p, :, :LANES] = t0
        s.nrmp[2 * p, :, LANES:] = t1
        s.nrmp[2 * p + 1, :, :LANES] = swap(jnp.where(low8, t2, t1))
        s.nrmp[2 * p + 1, :, LANES:] = swap(t2)
    red.start_norm()
    grad_tiles = []
    factor = s.rstd[...]
    for n in range(width // LANES):
        cols = slice(n * LANES, (n + 1) * LANES)
        grad_tiles.append(factor * (
            s.comb[:, cols] - back1 / width - s.normed[:, cols] * (back2 / width)))
    put_tiles(s.gradp, grad_tiles)
    red.start_grad()

    red.outputs_out()
    red.finish(0)
    for t in red.order:
        red.stage_row(2, t)
    red.outputs_grad()
    red.finish(1)
    red.norm_rows()
    red.spread(0)
    for n, t in enumerate(red.order):
        red.stage_row(3, t)
        if n == 1:
            red.norm_cols()
        if n == last:
            red.finish(2)
    red.grads_home()
    red.spread(1)
    red.finish(3)
    red.norm_last()
    red.spread(2)
    red.spread(3)
    gat.drain()
    red.drain()


LISTS = ("whole", "part", "crecv", "fsend", "frecv", "zsend", "zrecv", "extra")


def layer_all(row_count, data_count, width, tok, cot, nrm, segs, freq, own):
    n = row_count
    bf16, f32 = jnp.bfloat16, jnp.float32
    dma = pltpu.SemaphoreType.DMA
    vmem = pl.BlockSpec(memory_space=pltpu.VMEM)
    anywhere = pl.BlockSpec(memory_space=pl.ANY)
    shares, rows, _ = tok.shape
    length = segs.shape[1]
    groups = len(own)
    groups_out = data_count // QUARTERS
    sizes = [w.shape[1] for w in own]
    local = own[0].shape[0]
    depth = local // QUARTERS
    block = (rows, LANES)
    small = nrm.shape
    attn, hidden = sizes[1], sizes[3]
    spec = {}

    def buffers(dtype, **shapes):
        for name, shape in shapes.items():
            spec[name] = pltpu.VMEM(shape, dtype)

    def each(name, lead):
        for g, size in enumerate(sizes):
            spec[f"{name}{g}"] = pltpu.VMEM(lead + (size,), bf16)

    def sems(**shapes):
        for name, shape in shapes.items():
            spec[name] = dma(shape)

    each("whole", (width,))
    each("part", (width,))
    each("crecv", (2, n, depth))
    for name in ("fsend", "frecv", "zsend", "zrecv"):
        each(name, (n, depth))
    each("extra", (groups_out, depth))
    buffers(bf16, xg=(n,) + block, cg=(n,) + block, hop=(shares,) + block,
            fi=(length, width), si=(length, width), co=(length, width),
            fit=(width, length), sit=(width, length), cot=(width, length),
            dcat=(length, attn), att=(length, attn), act=(length, hidden), hg=(length, hidden),
            pg=(length, sizes[0]), outp=(n,) + block, gradp=(n,) + block,
            oy=(n,) + block, od=(n,) + block, gy=(n,) + block, gd=(n,) + block,
            gh=(shares,) + block)
    buffers(f32, ng=(n,) + small, nrmp=(n,) + small, nz=(n,) + small, nc=small, nrm1=small,
            nrm2=small, nd=(data_count,) + small, mask=(length // QBLOCK, QBLOCK, WINDOW + QBLOCK),
            cosine=(length, LANES), sine=(length, LANES), rstd=(length, LANES),
            dk=(length, LANES), dv=(length, LANES), normed=(length, width),
            comb=(length, width))
    sems(nrm_s=(n,), nrm_r=(n,), x_s=(shares,), x_r=(n,), xy_s=(n,), xy_r=(n,),
         h_s=(shares,), h_r=(shares,), c_s=(shares,), c_r=(n,), cy_s=(n,), cy_r=(n,),
         loc=(5,), own_l=(groups,), z_s=(2, groups, n), z_r=(groups, n),
         f_s=(groups, n), f_r=(groups, n), m_s=(2, groups, n), m_r=(2, groups, n),
         oy_s=(n,), oy_r=(n,), oz_s=(n,), oz_r=(shares,), gy_s=(n,), gy_r=(n,),
         gz_s=(n,), gz_r=(shares,), gh_s=(shares,), gh_r=(shares,), nz_s=(n,), nz_r=(n,),
         nc_s=(1,), nc_r=(1,), nd_s=(data_count,), nd_r=(data_count,),
         pc_s=(2, groups, n), pc_r=(2, groups, n), pf_s=(groups, n), pf_r=(groups, n),
         pz_s=(groups, n), pz_r=(groups, n), e_s=(groups, groups_out), e_r=(groups, groups_out),
         a_s=(groups,), a_r=(groups,), b_s=(2, groups), b_r=(2, groups))
    return pl.pallas_call(
        functools.partial(layer_kernel, n, width, groups_out, tuple(spec)),
        out_shape=[
            jax.ShapeDtypeStruct((shares,) + block, bf16),
            jax.ShapeDtypeStruct((shares,) + block, bf16),
            jax.ShapeDtypeStruct(small, f32),
        ] + [jax.ShapeDtypeStruct((local, size), bf16) for size in sizes],
        in_specs=[anywhere] * 3 + [vmem] * 2 + [anywhere] * groups,
        out_specs=[vmem] * (3 + groups),
        scratch_shapes=list(spec.values()),
        compiler_params=pltpu.CompilerParams(
            collective_id=0, has_side_effects=True, vmem_limit_bytes=63 << 20
        ),
        name="layer",
    )(tok, cot, nrm, segs, freq, *own)


def pack_tokens(rows, length):
    blocks = rows.reshape(-1, length, rows.shape[1])
    ends = blocks[:, :, LANES:]
    joined = jnp.concatenate([ends[:, :length // 2], ends[:, length // 2:]], 2)
    return jnp.concatenate([blocks[:, :, :LANES], joined], 1)


def unpack_tokens(blocks, length):
    joined = blocks[:, length:]
    small = joined.shape[2] // 2
    ends = jnp.concatenate([joined[:, :, :small], joined[:, :, small:]], 1)
    return jnp.concatenate([blocks[:, :length], ends], 2).reshape(-1, LANES + small)


def on_device(
    tokens_in,
    out_cot,
    segments,
    norm_params,
    qkv_weight,
    proj_weight,
    up_weight,
    down_weight,
    norm_first,
    norm_second,
    qkv_first,
    qkv_second,
    proj_first,
    proj_second,
    up_first,
    up_second,
    down_first,
    down_second,
):
    row_count = lax.axis_size("row")
    data_count = lax.axis_size("dp")
    col_count = lax.axis_size("col")
    local_count, local_width = tokens_in.shape
    width = local_width * row_count
    length = segments.shape[1]
    shares = local_count // length
    bf16 = jnp.bfloat16

    own = (
        qkv_weight.astype(bf16),
        proj_weight.T.astype(bf16),
        down_weight.T.astype(bf16),
        up_weight.astype(bf16),
    )
    nrm = jnp.pad(norm_params, ((0, 4), (0, 2 * LANES - local_width)))
    half = ROT_DIM // 2
    freq = rotary_base ** (-2.0 * jnp.arange(half, dtype=jnp.float32) / ROT_DIM)
    freq = jnp.concatenate([freq, freq, jnp.zeros(HEAD_DIM - ROT_DIM, jnp.float32)])
    freq = jnp.broadcast_to(jnp.tile(freq, 2)[None], (8, LANES))
    out_sum, grad_sum, norm_sum, qkv_sum, proj_sum, down_sum, up_sum = layer_all(
        row_count, data_count, width, pack_tokens(tokens_in, length),
        pack_tokens(out_cot, length), nrm, segments, freq, own)

    output = (tokens_in.astype(jnp.float32)
              + unpack_tokens(out_sum, length).astype(jnp.float32)).astype(bf16)
    input_grad = (out_cot.astype(jnp.float32)
                  + unpack_tokens(grad_sum, length).astype(jnp.float32)).astype(bf16)
    norm_grad = norm_sum[:4, :local_width]
    qkv_grad = qkv_sum.astype(jnp.float32)
    up_grad = up_sum.astype(jnp.float32)
    proj_grad = proj_sum.astype(jnp.float32).T
    down_grad = down_sum.astype(jnp.float32).T
    norm_new, norm_first_new, norm_second_new = adam_update(
        norm_params, norm_first, norm_second, norm_grad, 0.0
    )
    qkv_new, qkv_first_new, qkv_second_new = adam_update(
        qkv_weight, qkv_first, qkv_second, qkv_grad, decay_rate
    )
    proj_new, proj_first_new, proj_second_new = adam_update(
        proj_weight, proj_first, proj_second, proj_grad, decay_rate
    )
    up_new, up_first_new, up_second_new = adam_update(
        up_weight, up_first, up_second, up_grad, decay_rate
    )
    down_new, down_first_new, down_second_new = adam_update(
        down_weight, down_first, down_second, down_grad, decay_rate
    )
    return (
        output,
        input_grad,
        norm_grad,
        qkv_grad,
        proj_grad,
        up_grad,
        down_grad,
        norm_new,
        qkv_new,
        proj_new,
        up_new,
        down_new,
        norm_first_new,
        norm_second_new,
        qkv_first_new,
        qkv_second_new,
        proj_first_new,
        proj_second_new,
        up_first_new,
        up_second_new,
        down_first_new,
        down_second_new,
    )


def solution(mesh):
    placed = (
        P(("dp", "col"), "row"),
        P(("dp", "col"), "row"),
        P("dp", None),
        P(None, "row"),
        P("row", "col"),
        P("col", "row"),
        P("row", "col"),
        P("col", "row"),
        P(None, "row"),
        P(None, "row"),
        P("row", "col"),
        P("row", "col"),
        P("col", "row"),
        P("col", "row"),
        P("row", "col"),
        P("row", "col"),
        P("col", "row"),
        P("col", "row"),
    )
    return jax.shard_map(
        on_device,
        mesh=mesh,
        in_specs=placed,
        out_specs=(
            P(("dp", "col"), "row"),
            P(("dp", "col"), "row"),
            P(None, "row"),
            P("row", "col"),
            P("col", "row"),
            P("row", "col"),
            P("col", "row"),
            P(None, "row"),
            P("row", "col"),
            P("col", "row"),
            P("row", "col"),
            P("col", "row"),
            P(None, "row"),
            P(None, "row"),
            P("row", "col"),
            P("row", "col"),
            P("col", "row"),
            P("col", "row"),
            P("row", "col"),
            P("row", "col"),
            P("col", "row"),
            P("col", "row"),
        ),
        check_vma=False,
    )
```
